32 devices in a mesh: ctx: 4 (over z), pipe: 2 (over x), tp: 4 (over y, core).
Axes of the slice: x: 2, y: 2, z: 4, core: 2. Of those that a mesh axis runs over, the one named last changes fastest.
Arguments:
- upstream: bfloat16 [2, 512, 2688], P('pipe', 'ctx', 'tp'), may hold values from -6 to 6
- saved_input: bfloat16 [2, 512, 2688], P('pipe', 'ctx', 'tp'), may hold values from -0.59765625 to 0.59765625
- inv_rms: float32 [2, 512], P('pipe', 'ctx'), may hold values from 2 to 20
- norm_gain: float32 [2, 2688], P('pipe', 'tp'), may hold values from 0.1 to 1.9
- query_proj: bfloat16 [2, 512, 2048], P('pipe', 'ctx', 'tp'), may hold values from -14 to 14
- key_proj: bfloat16 [2, 512, 1024], P('pipe', 'ctx', 'tp'), may hold values from -5.2 to 5.2
- stored_value_rows: bfloat16 [2, 512, 1024], P('pipe', 'ctx', 'tp'), may hold values from -6 to 6
- attn_out: bfloat16 [2, 512, 2048], P('pipe', 'ctx', 'tp'), may hold values from -6 to 6
- w_query: bfloat16 [2, 2688, 2048], P('pipe', None, 'tp'), may hold values from -0.125 to 0.125
- key_projection_weight: bfloat16 [2, 2688, 1024], P('pipe', None, 'tp'), may hold values from -0.125 to 0.125
- value_projection_weight: bfloat16 [2, 2688, 1024], P('pipe', None, 'tp'), may hold values from -0.125 to 0.125
- w_out: bfloat16 [2, 2048, 2688], P('pipe', 'tp'), may hold values from -0.125 to 0.125
- seq_lengths: int32 [2], P('pipe'), may hold values from 256 to 512, as said below
Outputs:
- next_grad: bfloat16 [2, 512, 2688], P('pipe', 'ctx', 'tp')
The draws below stay inside these ranges and needn't reach their ends.
Inputs may be any that keep to these rules, and one draw needn't show every extreme that they name: `seq_lengths`: valid tokens come first in each sequence; at least one section's sequence has all 512 tokens valid.
All inputs are finite; a program needn't handle non-finite values.
Results may differ from the reference program's by a relative error of at most 0.0062.
Values may be sent and summed in bfloat16 or wider, within the bound.
A program may use at most 64 MiB of HBM per device.

```python
import math
import jax
import jax.numpy as jnp
from jax import lax

MODEL_WIDTH = 2688
QUERY_HEADS = 16
KEY_VALUE_HEADS = 8
HEAD_SIZE = 128
WINDOW = 1024
QUERY_SCALAR = 168
TOK_DEV = 128
RELAY_SECTIONS = 2
SEQUENCE_TOKENS = 512


def joint_projections(key):
    query_group_width = QUERY_HEADS // KEY_VALUE_HEADS
    key_start_row = jax.random.fold_in(key, 101)
    query_start_row = jax.random.fold_in(key, 202)
    key_entries = jnp.clip(jax.random.normal(key_start_row, (RELAY_SECTIONS, SEQUENCE_TOKENS, KEY_VALUE_HEADS, HEAD_SIZE), jnp.float32), -4.0, 4.0)
    query_entries = jnp.clip(jax.random.normal(query_start_row, (RELAY_SECTIONS, SEQUENCE_TOKENS, KEY_VALUE_HEADS, query_group_width, HEAD_SIZE), jnp.float32), -4.0, 4.0)
    return (query_entries.reshape(RELAY_SECTIONS, SEQUENCE_TOKENS, QUERY_HEADS * HEAD_SIZE), key_entries.reshape(RELAY_SECTIONS, SEQUENCE_TOKENS, KEY_VALUE_HEADS * HEAD_SIZE))


def draw_query_proj(key, part):
    return joint_projections(key)[0].astype(jnp.bfloat16)


def draw_key_proj(key, part):
    return joint_projections(key)[1].astype(jnp.bfloat16)


def draw_seq_lengths(key, part):
    first_key = jax.random.fold_in(key, 505)
    second_key = jax.random.fold_in(key, 606)
    lengths_drawn = jax.random.randint(first_key, (RELAY_SECTIONS,), SEQUENCE_TOKENS // 2, SEQUENCE_TOKENS + 1)
    chosen = jax.random.randint(second_key, (), 0, RELAY_SECTIONS)
    return jnp.where(jnp.arange(RELAY_SECTIONS) == chosen, SEQUENCE_TOKENS, lengths_drawn).astype(jnp.int32)


def block_scale(key, extent, split, least, top_value):
    gain, own = 1.0, jax.random.fold_in(key, 6)
    for dim, shards_of in split:
        heights = jnp.exp(jax.random.uniform(jax.random.fold_in(own, dim), (shards_of,), jnp.float32, least / len(split), top_value / len(split)))
        gain = gain * jnp.repeat(heights, extent[dim] // shards_of).reshape([-1 if axis == dim else 1 for axis in range(len(extent))])
    return gain


def normal_values(stream_key, shape, deviation, limit, split=(), kind=jnp.bfloat16):
    drawn = deviation * jax.random.normal(stream_key, shape, jnp.float32)
    if split:
        drawn = drawn * block_scale(stream_key, shape, split, -0.22, 0.18)
    return jnp.clip(drawn, -limit, limit).astype(kind)


def setup_inputs(seed: int = 0) -> dict:
    seeds = jax.random.split(jax.random.key(seed), 14)
    return {
        "upstream": normal_values(seeds[0], (RELAY_SECTIONS, SEQUENCE_TOKENS, MODEL_WIDTH), 1.0, 6.0, ((0, 2), (1, 4), (2, 4))),
        "saved_input": normal_values(seeds[1], (RELAY_SECTIONS, SEQUENCE_TOKENS, MODEL_WIDTH), 0.1, 0.59765625, ((0, 2), (1, 4), (2, 4))),
        "inv_rms": jnp.clip(jnp.exp(math.log(20.0) - 2.3025851 * jax.random.uniform(seeds[2], (RELAY_SECTIONS, SEQUENCE_TOKENS), jnp.float32) ** block_scale(seeds[2], (RELAY_SECTIONS, SEQUENCE_TOKENS), ((0, 2), (1, 4)), -0.2, 0.2)), 2.0, 20.0),
        "norm_gain": jnp.clip(1.0 + 0.18 * jax.random.normal(seeds[3], (RELAY_SECTIONS, MODEL_WIDTH), jnp.float32), 0.1, 1.9),
        "query_proj": draw_query_proj(jax.random.fold_in(seeds[13], 71), 0),
        "key_proj": draw_key_proj(jax.random.fold_in(seeds[13], 71), 0),
        "stored_value_rows": normal_values(seeds[6], (RELAY_SECTIONS, SEQUENCE_TOKENS, KEY_VALUE_HEADS * HEAD_SIZE), 1.0, 6.0, ((0, 2), (1, 4), (2, 4))),
        "attn_out": normal_values(seeds[7], (RELAY_SECTIONS, SEQUENCE_TOKENS, QUERY_HEADS * HEAD_SIZE), 1.0, 6.0, ((0, 2), (1, 4), (2, 4))),
        "w_query": normal_values(seeds[8], (RELAY_SECTIONS, MODEL_WIDTH, QUERY_HEADS * HEAD_SIZE), MODEL_WIDTH ** -0.5, 0.125, ((0, 2), (2, 4))),
        "key_projection_weight": normal_values(seeds[9], (RELAY_SECTIONS, MODEL_WIDTH, KEY_VALUE_HEADS * HEAD_SIZE), MODEL_WIDTH ** -0.5, 0.125, ((0, 2), (2, 4))),
        "value_projection_weight": normal_values(seeds[10], (RELAY_SECTIONS, MODEL_WIDTH, KEY_VALUE_HEADS * HEAD_SIZE), MODEL_WIDTH ** -0.5, 0.125, ((0, 2), (2, 4))),
        "w_out": normal_values(seeds[11], (RELAY_SECTIONS, QUERY_HEADS * HEAD_SIZE, MODEL_WIDTH), (QUERY_HEADS * HEAD_SIZE) ** -0.5, 0.125, ((0, 2), (1, 4))),
        "seq_lengths": draw_seq_lengths(jax.random.fold_in(seeds[13], 71), 0),
    }


NEG_FILL = -1.0e30
CONTRACT_LAST = (((1,), (1,)), ((), ()))


def window_mask(pos_query, pos_key, length):
    later = pos_query[:, None] - pos_key[None, :]
    inside = (later >= 0) & (later < WINDOW) & (pos_key[None, :] >= 0)
    return inside & (pos_key[None, :] < length) & (pos_query[:, None] < length)


def block_grads(query_block_rows, output_grad_block, output_block, key_block_rows, value_block_rows, pos_query, pos_key, length):
    score_scale = QUERY_SCALAR ** -0.5
    query_group_width = QUERY_HEADS // KEY_VALUE_HEADS
    block_row_count = query_block_rows.shape[0]
    key_total_count = key_block_rows.shape[0]
    query_head_rows = query_block_rows.astype(jnp.float32).reshape(block_row_count, KEY_VALUE_HEADS, query_group_width, HEAD_SIZE)
    output_grad_heads = output_grad_block.astype(jnp.float32).reshape(block_row_count, KEY_VALUE_HEADS, query_group_width, HEAD_SIZE)
    output_heads = output_block.astype(jnp.float32).reshape(block_row_count, KEY_VALUE_HEADS, query_group_width, HEAD_SIZE)
    key_head_rows = key_block_rows.astype(jnp.float32).reshape(key_total_count, KEY_VALUE_HEADS, HEAD_SIZE)
    value_head_rows = value_block_rows.astype(jnp.float32).reshape(key_total_count, KEY_VALUE_HEADS, HEAD_SIZE)
    allowed = window_mask(pos_query, pos_key, length)
    live_rows = pos_query < length
    scores = jnp.einsum('tgrd,kgd->grtk', query_head_rows, key_head_rows) * score_scale
    scores = jnp.where(allowed, scores, NEG_FILL)
    top_score = jnp.max(scores, axis=-1, keepdims=True)
    raised = jnp.where(allowed, jnp.exp(scores - top_score), 0.0)
    row_total = jnp.sum(raised, axis=-1, keepdims=True)
    weights = raised / jnp.where(live_rows[:, None], row_total, 1.0)
    output_dot_grad = jnp.einsum('uhap,uhap->hau', output_grad_heads, output_heads)
    dprob = jnp.einsum('tgrd,kgd->grtk', output_grad_heads, value_head_rows)
    dscore = (weights * (dprob - output_dot_grad[..., None])).astype(jnp.bfloat16)
    weights_low = weights.astype(jnp.bfloat16)
    dscore_wide = lax.optimization_barrier(dscore).astype(jnp.float32)
    weights_wide = lax.optimization_barrier(weights_low).astype(jnp.float32)
    query_gradient = (jnp.einsum('grtk,kgd->tgrd', dscore_wide, key_head_rows) * score_scale).astype(jnp.bfloat16)
    key_gradient = jnp.einsum('grtk,tgrd->kgd', dscore_wide, query_head_rows) * score_scale
    value_gradient = jnp.einsum('grtk,tgrd->kgd', weights_wide, output_grad_heads)
    return (query_gradient.reshape(block_row_count, QUERY_HEADS * HEAD_SIZE), key_gradient.reshape(key_total_count, KEY_VALUE_HEADS * HEAD_SIZE),
            value_gradient.reshape(key_total_count, KEY_VALUE_HEADS * HEAD_SIZE))


def section_grads(grad_in, inputs, inv_row, gain_row, queries, key_row_span, value_row_span, out_rows,
                weight_query, weight_key, weight_value, weight_out, length):
    reach = (WINDOW - 2 + TOK_DEV) // TOK_DEV
    border_rows = reach * TOK_DEV
    grad_out = lax.dot_general(grad_in, weight_out, CONTRACT_LAST,
                               preferred_element_type=jnp.float32).astype(jnp.bfloat16)
    key_with_padding = jnp.concatenate([jnp.zeros((border_rows, KEY_VALUE_HEADS * HEAD_SIZE), key_row_span.dtype), key_row_span], axis=0)
    value_with_padding = jnp.concatenate([jnp.zeros((border_rows, KEY_VALUE_HEADS * HEAD_SIZE), value_row_span.dtype), value_row_span], axis=0)

    def advance(carry, block_index):
        key_acc, value_acc = carry
        anchor = (block_index * TOK_DEV).astype(jnp.int32)
        pos_query = anchor + lax.iota(jnp.int32, TOK_DEV)
        pos_key = anchor - border_rows + lax.iota(jnp.int32, border_rows + TOK_DEV)
        query_gradient, key_gradient, value_gradient = block_grads(
            lax.dynamic_slice_in_dim(queries, anchor, TOK_DEV, 0),
            lax.dynamic_slice_in_dim(grad_out, anchor, TOK_DEV, 0),
            lax.dynamic_slice_in_dim(out_rows, anchor, TOK_DEV, 0),
            lax.dynamic_slice_in_dim(key_with_padding, anchor, border_rows + TOK_DEV, 0),
            lax.dynamic_slice_in_dim(value_with_padding, anchor, border_rows + TOK_DEV, 0),
            pos_query, pos_key, length)
        key_acc = lax.dynamic_update_slice_in_dim(
            key_acc, lax.dynamic_slice_in_dim(key_acc, anchor, border_rows + TOK_DEV, 0) + key_gradient, anchor, 0)
        value_acc = lax.dynamic_update_slice_in_dim(
            value_acc, lax.dynamic_slice_in_dim(value_acc, anchor, border_rows + TOK_DEV, 0) + value_gradient, anchor, 0)
        return (key_acc, value_acc), query_gradient

    initial_totals = jnp.zeros((border_rows + SEQUENCE_TOKENS, KEY_VALUE_HEADS * HEAD_SIZE), jnp.float32)
    (key_acc, value_acc), query_blocks = lax.scan(
        advance, (initial_totals, initial_totals), jnp.arange(SEQUENCE_TOKENS // TOK_DEV, dtype=jnp.int32))
    query_gradient = query_blocks.reshape(SEQUENCE_TOKENS, QUERY_HEADS * HEAD_SIZE)
    key_gradient = key_acc[border_rows:].astype(jnp.bfloat16)
    value_gradient = value_acc[border_rows:].astype(jnp.bfloat16)
    normed_grad = (lax.dot_general(query_gradient, weight_query, CONTRACT_LAST, preferred_element_type=jnp.float32)
                   + lax.dot_general(key_gradient, weight_key, CONTRACT_LAST, preferred_element_type=jnp.float32)
                   + lax.dot_general(value_gradient, weight_value, CONTRACT_LAST, preferred_element_type=jnp.float32))
    coupling = (jnp.sum(query_gradient.astype(jnp.float32) * queries.astype(jnp.float32), axis=1)
                + jnp.sum(key_gradient.astype(jnp.float32) * key_row_span.astype(jnp.float32), axis=1)
                + jnp.sum(value_gradient.astype(jnp.float32) * value_row_span.astype(jnp.float32), axis=1))
    scale_rows = inv_row[:, None]
    result = grad_in.astype(jnp.float32) + scale_rows * (
        gain_row[None, :] * normed_grad - inputs.astype(jnp.float32) * scale_rows * coupling[:, None] / MODEL_WIDTH)
    return result.astype(jnp.bfloat16)


def reference(upstream, saved_input, inv_rms, norm_gain, query_proj, key_proj, stored_value_rows, attn_out,
              w_query, key_projection_weight, value_projection_weight, w_out, seq_lengths):
    results = []
    for section in range(RELAY_SECTIONS):
        results.append(section_grads(upstream[section], saved_input[section], inv_rms[section], norm_gain[section],
                                   query_proj[section], key_proj[section], stored_value_rows[section], attn_out[section],
                                   w_query[section], key_projection_weight[section], value_projection_weight[section], w_out[section],
                                   seq_lengths[section]))
    stacked = jnp.stack(results, axis=0)
    return jnp.roll(stacked, -1, axis=0)
```

```python
import functools

import jax
import jax.numpy as jnp
from jax import lax
from jax.experimental import pallas as pl
from jax.experimental.pallas import tpu as pltpu
from jax.sharding import PartitionSpec as P

QUERY_HEADS = 16
KEY_VALUE_HEADS = 8
HEAD_SIZE = 128
WINDOW = 1024
QUERY_SCALAR = 168
NEG_FILL = -1e30
GATHER_ROWS = 256
COUPLING_ROWS = 16
NT = (((1,), (1,)), ((), ()))
NN = (((1,), (0,)), ((), ()))
TN = (((0,), (0,)), ((), ()))
BF = jnp.bfloat16
F32 = jnp.float32


def chunk_count(width):
    for n in (6, 4, 3, 2):
        if width % (16 * n) == 0:
            return n
    return 1


def gather_cuts(width):
    return [(at, min(GATHER_ROWS, width - at)) for at in range(0, width, GATHER_ROWS)]


def chunk_groups(chunks):
    groups, first, count = [], 0, 1
    while first < chunks:
        count = min(count, chunks - first)
        groups.append((first, count))
        first, count = first + count, count + 1
    return groups


def direct_reach(reach):
    return [d for d in range(1, reach + 1) if d != 2]


def far_reach(reach):
    return [d for d in direct_reach(reach) if reach >= 2]


def dot(a, b, dims):
    return lax.dot_general(a, b, dims, preferred_element_type=F32)


def kernel(
    ctx_n,
    pipe_n,
    reach,
    up_h,
    xin_h,
    inv_h,
    gain_h,
    q_h,
    k_h,
    v_h,
    ao_h,
    wq_h,
    wk_h,
    wv_h,
    wo_h,
    len_h,
    out_h,
    gath,
    xin,
    inv,
    gain,
    q,
    kb,
    vb,
    ao,
    wq,
    wk,
    wv,
    wo,
    slen,
    wo_cut,
    gain_col,
    ao_t,
    q_t,
    k_t,
    do_t,
    stat,
    s,
    dp,
    ds,
    q_far,
    do_far,
    stat_far,
    s_far,
    part_v,
    part_k,
    snd,
    rcv,
    pacc,
    rs_a,
    rs_ar,
    rs_b,
    rs_br,
    rs_c,
    rs_cr,
    res,
    lsem,
    k_s,
    k_r,
    v_s,
    v_r,
    ag_s,
    ag_r,
    q_s,
    q_r,
    do_s,
    do_r,
    st_s,
    st_r,
    acc_s,
    acc_r,
    rs_s,
    rs_rv,
    x_s,
    x_r,
):
    i = lax.axis_index("ctx")
    p = lax.axis_index("pipe")
    t = lax.axis_index("tp")
    partner = t + 1 - 2 * (t % 2)
    cross = (t + 2) % 4
    diag = 3 - t
    rows = q.shape[0]
    width = xin.shape[0]
    kv_heads = kb.shape[1] // HEAD_SIZE
    group = q.shape[1] // kb.shape[1]
    stacked = group * rows
    scale = QUERY_SCALAR ** (-0.5)
    model_width = width * 4
    chunks = chunk_count(width)
    chunk = width // chunks
    cuts = gather_cuts(width)
    direct = direct_reach(reach)
    far = far_reach(reach)

    def local(src, dst, n):
        c = pltpu.make_async_copy(src, dst, lsem.at[n])
        c.start()
        return c

    def remote(src, dst, ss, rs, dev):
        return pltpu.make_async_remote_copy(
            src_ref=src,
            dst_ref=dst,
            send_sem=ss,
            recv_sem=rs,
            device_id=dev,
            device_id_type=pl.DeviceIdType.MESH,
        )

    barrier = pltpu.get_barrier_semaphore()

    def greet(dev):
        pl.semaphore_signal(
            barrier, inc=1, device_id=dev, device_id_type=pl.DeviceIdType.MESH
        )

    has_up = i + 1 < ctx_n
    has_down = i > 0

    greet({"tp": cross})
    greet({"tp": partner})
    expect = 2
    for d in direct:

        @pl.when(i + d < ctx_n)
        def _():
            greet({"ctx": i + d})

        @pl.when(i >= d)
        def _():
            greet({"ctx": i - d})

        expect = expect + jnp.where(i + d < ctx_n, 1, 0) + jnp.where(i >= d, 1, 0)
    prev = (p + pipe_n - 1) % pipe_n
    if pipe_n > 1:
        greet({"pipe": prev})
        expect += 1
    if pipe_n > 2:
        greet({"pipe": (p + 1) % pipe_n})
        expect += 1

    c_q = local(q_h, q, 1)
    c_k = local(k_h, kb.at[pl.ds(0, rows)], 0)
    c_len = local(len_h, slen, 2)
    c_up = local(up_h, gath.at[t], 3)
    c_wo = local(wo_h, wo, 5)
    c_ao = local(ao_h, ao, 6)
    c_gain = local(gain_h, gain, 12)
    c_v = local(v_h, vb.at[pl.ds(0, rows)], 4)
    c_wq = local(wq_h, wq, 7)
    c_wk = local(wk_h, wk, 8)
    c_wv = local(wv_h, wv, 9)
    c_xin = local(xin_h, xin, 10)
    c_inv = local(inv_h, inv, 11)

    def head_cols(h):
        return slice(h * HEAD_SIZE, (h + 1) * HEAD_SIZE)

    def block_rows(d):
        return slice(d * rows, (d + 1) * rows)

    def flip(x):
        return x.astype(F32).T

    c_q.wait()
    for g in range(kv_heads):
        for r in range(group):
            q_t[g, :, block_rows(r)] = flip(q[:, head_cols(g * group + r)]).astype(BF)

    pl.semaphore_wait(barrier, expect)

    def kv_copy(src_h, buf, ss, rs, d):
        dst = buf.at[pl.ds(d * rows, rows)]
        if d == 2:
            return remote(buf.at[pl.ds(rows, rows)], dst, ss.at[d], rs.at[d], {"ctx": i + 1})
        return remote(src_h, dst, ss.at[d], rs.at[d], {"ctx": i + d})

    def k_copy(d):
        return kv_copy(k_h, kb, k_s, k_r, d)

    def v_copy(d):
        return kv_copy(v_h, vb, v_s, v_r, d)

    def sends_up(d):
        return has_up & has_down if d == 2 else i + d < ctx_n

    def q_copy(n):
        return remote(q_t, q_far.at[n], q_s.at[n], q_r.at[n], {"ctx": i - far[n]})

    def do_copy(n, g):
        return remote(
            do_t.at[g], do_far.at[n, g], do_s.at[n, g], do_r.at[n, g], {"ctx": i - far[n]}
        )

    def stat_copy(n):
        return remote(stat, stat_far.at[n], st_s.at[n], st_r.at[n], {"ctx": i - far[n]})

    def sends_far(n):
        return i >= 2 if far[n] == 1 else i >= far[n]

    def takes_far(n):
        return has_up & has_down if far[n] == 1 else i + far[n] < ctx_n

    def acc_copy(g):
        return remote(snd.at[g], rcv.at[g], acc_s.at[g], acc_r.at[g], {"ctx": i - 1})

    parts = len(cuts)

    def ag_cross(n):
        sl = pl.ds(*cuts[n])
        return remote(up_h.at[sl], gath.at[t, sl], ag_s.at[n], ag_r.at[n], {"tp": cross})

    def ag_fwd(n):
        sl = pl.ds(*cuts[n])
        m = parts + n
        return remote(
            gath.at[cross, sl], gath.at[cross, sl], ag_s.at[m], ag_r.at[m], {"tp": partner}
        )

    ag_part = remote(
        up_h, gath.at[t], ag_s.at[2 * parts], ag_r.at[2 * parts], {"tp": partner}
    )
    for n in range(parts):
        ag_cross(n).start()
    for d in direct:

        @pl.when(sends_up(d))
        def _():
            k_copy(d).start()

    for n in range(len(far)):

        @pl.when(sends_far(n))
        def _():
            q_copy(n).start()

    ag_part.start()
    for d in direct:

        @pl.when(sends_up(d))
        def _():
            v_copy(d).start()

    for d in range(1, reach + 1):

        @pl.when(i < d)
        def _():
            kb[block_rows(d)] = jnp.zeros((rows, kb.shape[1]), BF)
            vb[block_rows(d)] = jnp.zeros((rows, vb.shape[1]), BF)

    c_len.wait()
    length = slen[0]
    key_i = lax.broadcasted_iota(jnp.int32, (rows, stacked), 0)
    qry_i = lax.broadcasted_iota(jnp.int32, (rows, stacked), 1) % rows
    later0 = qry_i - key_i
    pos_q = i * rows + qry_i
    live = (pos_q < length)[:1]

    def allowed(query_pos, d):
        later = later0 + d * rows
        pos_k = query_pos - later
        ok = (later >= 0) & (later < WINDOW) & (pos_k < length) & (query_pos < length)
        return ok & (pos_k >= 0)

    def scores(d):
        ok = allowed(pos_q, d)
        for g in range(kv_heads):
            keys = kb[block_rows(d), head_cols(g)]
            sc = dot(keys, q_t[g], NN) * scale
            s[g, block_rows(d)] = jnp.where(ok, sc, NEG_FILL)
            k_t[g, :, block_rows(d)] = flip(keys).astype(BF)

    c_k.wait()
    scores(0)
    c_wo.wait()
    for n in range(4):
        wo_cut[n] = wo[:, n * width : (n + 1) * width]
    c_ao.wait()
    for h in range(kv_heads * group):
        ao_t[head_cols(h), :] = flip(ao[:, head_cols(h)])
    c_gain.wait()
    gain_col[...] = jnp.broadcast_to(gain[...], (rows, width)).T

    c_up.wait()
    acc = dot(wo_cut[t], gath[t], NN)
    ag_part.wait_recv()
    acc = acc + dot(wo_cut[partner], gath[partner], NN)

    def take(copy, d):
        @pl.when(i >= d)
        def _():
            copy(d).wait_recv()

    def pass_on(copy):
        if reach >= 2:

            @pl.when(sends_up(2))
            def _():
                copy(2).start()

    if reach >= 1:
        take(k_copy, 1)
        pass_on(k_copy)
        scores(1)

    for n, (at, size) in enumerate(cuts):
        ag_cross(n).wait_recv()
        ag_fwd(n).start()
        acc = acc + dot(wo_cut[cross, :, at : at + size], gath[cross, at : at + size], NN)
    if reach >= 1:
        take(v_copy, 1)
        pass_on(v_copy)
    for n, (at, size) in enumerate(cuts):
        ag_fwd(n).wait_recv()
        acc = acc + dot(wo_cut[diag, :, at : at + size], gath[diag, at : at + size], NN)
    grad = acc.astype(BF)
    for g in range(kv_heads):
        for r in range(group):
            do_t[g, :, block_rows(r)] = grad[head_cols(g * group + r)]

    def send_dout(n):
        @pl.when(sends_far(n))
        def _():
            for g in range(kv_heads):
                do_copy(n, g).start()

    def send_stat(n):
        @pl.when(sends_far(n))
        def _():
            stat_copy(n).start()

    if far:
        send_dout(0)

    for g in range(kv_heads):
        sums = []
        for r in range(group):
            h = g * group + r
            sums.append(
                jnp.sum(
                    grad[head_cols(h)].astype(F32) * ao_t[head_cols(h), :], axis=0, keepdims=True
                )
            )
        stat[3 * g + 2 : 3 * g + 3, :] = jnp.concatenate(sums, axis=1)

    for d in range(2, reach + 1):
        take(k_copy, d)
        scores(d)

    for g in range(kv_heads):
        top = jnp.max(s[g], axis=0, keepdims=True)
        total = jnp.zeros((1, stacked), F32)
        for d in range(reach + 1):
            e = jnp.exp(s[g, block_rows(d)] - top)
            s[g, block_rows(d)] = e
            total = total + jnp.sum(e, axis=0, keepdims=True)
        inv_total = jnp.where(live, 1.0 / total, 0.0)
        for d in range(reach + 1):
            s[g, block_rows(d)] = s[g, block_rows(d)] * inv_total
        stat[3 * g : 3 * g + 1, :] = top
        stat[3 * g + 1 : 3 * g + 2, :] = inv_total

    if far:
        send_stat(0)
    for n in range(1, len(far)):
        send_dout(n)
        send_stat(n)

    c_v.wait()
    for d in range(2, reach + 1):
        take(v_copy, d)

    own = min(reach, 1) + 1
    for g in range(kv_heads):
        dp[g] = dot(vb[:, head_cols(g)], do_t[g], NN)
        part_v[g] = dot(s[g, : own * rows].astype(BF), do_t[g], NT)
        delta = stat[3 * g + 2 : 3 * g + 3, :]
        for d in range(reach + 1):
            ds[g, block_rows(d)] = (
                s[g, block_rows(d)] * (dp[g, block_rows(d)] - delta)
            ).astype(BF)
        part_k[g] = dot(ds[g, : own * rows], q_t[g], NT)

    def send_acc(g):
        snd[g, :rows] = part_v[g, block_rows(1)].astype(BF)
        snd[g, rows:] = part_k[g, block_rows(1)].astype(BF)
        acc_copy(g).start()

    if reach >= 1:

        @pl.when(has_down & jnp.logical_not(has_up) if reach >= 2 else has_down)
        def _():
            for g in range(kv_heads):
                send_acc(g)

    coupling = jnp.zeros((1, rows), F32)
    low = []
    for g in range(kv_heads):
        dq = dot(k_t[g], ds[g], NN) * scale
        for r in range(group):
            part = dq[:, block_rows(r)].astype(BF)
            low.append(part)
            coupling = coupling + jnp.sum(
                part.astype(F32) * q_t[g, :, block_rows(r)].astype(F32), axis=0, keepdims=True
            )
    dq_low = jnp.concatenate(low, axis=0)
    owners = (diag, cross, partner, t)

    def piece_rows(n, at=0, size=width):
        return pl.ds(pl.multiple_of(owners[n] * width + at, 16), size)

    def far_scores(n):
        e = far[n]
        kd, dist = (1, 2) if e == 1 else (0, e)

        @pl.when(takes_far(n))
        def _():
            q_copy(n).wait_recv()
            ok = allowed((i + e) * rows + qry_i, dist)
            for g in range(kv_heads):
                sc = dot(kb[block_rows(kd), head_cols(g)], q_far[n, g], NN) * scale
                s_far[n, g] = jnp.where(ok, sc, NEG_FILL)

    def far_pair(n):
        e = far[n]
        kd = 1 if e == 1 else 0

        @pl.when(takes_far(n))
        def _():
            stat_copy(n).wait_recv()
            for g in range(kv_heads):
                top = stat_far[n, 3 * g : 3 * g + 1, :]
                inv_total = stat_far[n, 3 * g + 1 : 3 * g + 2, :]
                s_far[n, g] = jnp.exp(s_far[n, g] - top) * inv_total
            for g in range(kv_heads):
                delta = stat_far[n, 3 * g + 2 : 3 * g + 3, :]
                do_copy(n, g).wait_recv()
                part_v[g, block_rows(kd)] += dot(s_far[n, g].astype(BF), do_far[n, g], NT)
                dprob = dot(vb[block_rows(kd), head_cols(g)], do_far[n, g], NN)
                dsc = (s_far[n, g] * (dprob - delta)).astype(BF)
                part_k[g, block_rows(kd)] += dot(dsc, q_far[n, g], NT)
                if e == 1:
                    send_acc(g)

    if far:
        far_scores(0)
    c_wq.wait()
    for n in range(4):
        pacc[n] = dot(wq[piece_rows(n), :], dq_low, NN)
    if far:
        far_pair(0)
    for n in range(1, len(far)):
        far_scores(n)
    for n in range(1, len(far)):
        far_pair(n)
    c_wk.wait()
    c_wv.wait()
    c_xin.wait()
    c_inv.wait()
    if reach >= 1:

        @pl.when(has_up)
        def _():
            for g in range(kv_heads):
                acc_copy(g).wait_recv()
                part_v[g, :rows] += rcv[g, :rows].astype(F32)
                part_k[g, :rows] += rcv[g, rows:].astype(F32)

    dv_low = jnp.concatenate([part_v[g, :rows].astype(BF) for g in range(kv_heads)], axis=1)
    dk_low = jnp.concatenate(
        [(part_k[g, :rows] * scale).astype(BF) for g in range(kv_heads)], axis=1
    )
    both = dk_low.astype(F32) * kb[:rows].astype(F32) + dv_low.astype(F32) * vb[:rows].astype(F32)
    for g in range(kv_heads):
        coupling = coupling + jnp.sum(both[:, head_cols(g)].T, axis=0, keepdims=True)

    def piece(n, at=0, size=width):
        span = piece_rows(n, at, size)
        more = dot(wk[span, :], dk_low, NT) + dot(wv[span, :], dv_low, NT)
        return pacc[n, at : at + size] + more

    lead = COUPLING_ROWS
    wide = jnp.broadcast_to(coupling, (lead, rows))

    def span_of(n, count=1):
        return (0, lead + count * chunk) if n == 0 else (lead + n * chunk, count * chunk)

    groups = chunk_groups(chunks)

    def a_copy(m):
        sl = pl.ds(*span_of(*groups[m]))
        return remote(
            rs_a.at[sl], rs_ar.at[sl], rs_s.at[1 + m], rs_rv.at[1 + m], {"tp": partner}
        )

    send_c = remote(rs_c, rs_cr, rs_s.at[0], rs_rv.at[0], {"tp": partner})
    base = 1 + len(groups)

    def b_copy(n):
        sl = pl.ds(*span_of(n))
        return remote(
            rs_b.at[sl], rs_br.at[sl], rs_s.at[base + n], rs_rv.at[base + n], {"tp": cross}
        )

    def x_copy(n):
        sl = pl.ds(n * chunk, chunk)
        if pipe_n == 1:
            return pltpu.make_async_copy(res.at[sl], out_h.at[sl], x_s.at[n])
        return remote(res.at[sl], out_h.at[sl], x_s.at[n], x_r.at[n], {"pipe": prev})

    rs_a[:lead, :] = wide.astype(BF)
    for m, (first, count) in enumerate(groups):
        at, size = first * chunk, count * chunk
        rs_a[lead + at : lead + at + size, :] = piece(0, at, size).astype(BF)
        a_copy(m).start()
    for m, (first, count) in enumerate(groups):
        at, size = first * chunk, count * chunk
        pacc[1, at : at + size] = piece(1, at, size)
        a_copy(m).wait_recv()
        if m == 0:
            rs_b[:lead, :] = (wide + rs_ar[:lead, :].astype(F32)).astype(BF)
        for n in range(first, first + count):
            sl = slice(n * chunk, (n + 1) * chunk)
            sh = slice(lead + n * chunk, lead + (n + 1) * chunk)
            rs_b[sh, :] = (pacc[1, sl] + rs_ar[sh, :].astype(F32)).astype(BF)
            b_copy(n).start()
    rs_c[lead:, :] = piece(2).astype(BF)
    rs_c[:lead, :] = wide.astype(BF)
    send_c.start()
    pacc[3] = piece(3)
    iv = inv[...]
    send_c.wait_recv()
    for n in range(chunks):
        sl = slice(n * chunk, (n + 1) * chunk)
        sh = slice(lead + n * chunk, lead + (n + 1) * chunk)
        b_copy(n).wait_recv()
        if n == 0:
            coup = (
                coupling + rs_cr[:lead, :].astype(F32)[:1] + rs_br[:lead, :].astype(F32)[:1]
            )
            drag = iv * coup / model_width
        normed = pacc[3, sl] + rs_cr[sh, :].astype(F32) + rs_br[sh, :].astype(F32)
        val = gath[t, sl, :].astype(F32) + iv * (
            gain_col[sl, :] * normed - xin[sl, :].astype(F32) * drag
        )
        res[sl, :] = val.astype(BF)
        x_copy(n).start()

    for n in range(parts):
        ag_cross(n).wait_send()
        ag_fwd(n).wait_send()
    ag_part.wait_send()
    for d in range(1, reach + 1):

        @pl.when(sends_up(d))
        def _():
            k_copy(d).wait_send()
            v_copy(d).wait_send()

    for n in range(len(far)):

        @pl.when(sends_far(n))
        def _():
            q_copy(n).wait_send()
            stat_copy(n).wait_send()
            for g in range(kv_heads):
                do_copy(n, g).wait_send()

    if reach >= 1:

        @pl.when(has_down)
        def _():
            for g in range(kv_heads):
                acc_copy(g).wait_send()

    send_c.wait_send()
    for m in range(len(groups)):
        a_copy(m).wait_send()
    for n in range(chunks):
        b_copy(n).wait_send()
    for n in range(chunks):
        x_copy(n).wait()


def per_device(up, xin, inv, gain, q, k, v, ao, wq, wk, wv, wo, lens):
    ctx_n = lax.axis_size("ctx")
    pipe_n = lax.axis_size("pipe")
    tp_n = lax.axis_size("tp")
    assert tp_n == 4
    up, xin, q, k, v, ao = up[0].T, xin[0].T, q[0], k[0], v[0], ao[0]
    wq, wk, wv, wo = wq[0], wk[0], wv[0], wo[0]
    width, rows = up.shape
    reach = min((WINDOW - 2 + rows) // rows, ctx_n - 1)
    kv_cols, q_cols = k.shape[1], q.shape[1]
    kv_heads = kv_cols // HEAD_SIZE
    stacked = rows * (q_cols // kv_cols)
    chunks = chunk_count(width)
    groups = len(chunk_groups(chunks))
    parts = len(gather_cuts(width))
    vm = pltpu.VMEM
    dma = pltpu.SemaphoreType.DMA
    blocks = reach + 1
    own = min(reach, 1) + 1
    far = max(len(far_reach(reach)), 1)
    stats = -(-3 * kv_heads // 8) * 8
    scratch = [
        vm((tp_n, width, rows), BF),
        vm((width, rows), BF),
        vm(inv.shape, F32),
        vm(gain.shape, F32),
        vm(q.shape, BF),
        vm((blocks * rows, kv_cols), BF),
        vm((blocks * rows, kv_cols), BF),
        vm(ao.shape, BF),
        vm(wq.shape, BF),
        vm(wk.shape, BF),
        vm(wv.shape, BF),
        vm(wo.shape, BF),
        pltpu.SMEM(lens.shape, jnp.int32),
        vm((tp_n, wo.shape[0], width), BF),
        vm((width, rows), F32),
        vm((q_cols, rows), F32),
        vm((kv_heads, HEAD_SIZE, stacked), BF),
        vm((kv_heads, HEAD_SIZE, blocks * rows), BF),
        vm((kv_heads, HEAD_SIZE, stacked), BF),
        vm((stats, stacked), F32),
        vm((kv_heads, blocks * rows, stacked), F32),
        vm((kv_heads, blocks * rows, stacked), F32),
        vm((kv_heads, blocks * rows, stacked), BF),
        vm((far, kv_heads, HEAD_SIZE, stacked), BF),
        vm((far, kv_heads, HEAD_SIZE, stacked), BF),
        vm((far, stats, stacked), F32),
        vm((far, kv_heads, rows, stacked), F32),
        vm((kv_heads, own * rows, HEAD_SIZE), F32),
        vm((kv_heads, own * rows, HEAD_SIZE), F32),
        vm((kv_heads, 2 * rows, HEAD_SIZE), BF),
        vm((kv_heads, 2 * rows, HEAD_SIZE), BF),
        vm((tp_n, width, rows), F32),
    ]
    scratch += [vm((COUPLING_ROWS + width, rows), BF)] * 6
    scratch += [vm((width, rows), BF)]
    scratch += [dma((13,))]
    scratch += [dma((blocks,))] * 4
    scratch += [dma((2 * parts + 1,))] * 2
    scratch += [dma((far,))] * 2
    scratch += [dma((far, kv_heads))] * 2
    scratch += [dma((far,))] * 2
    scratch += [dma((kv_heads,))] * 2
    scratch += [dma((1 + groups + chunks,))] * 2
    scratch += [dma((chunks,))] * 2
    out = pl.pallas_call(
        functools.partial(kernel, ctx_n, pipe_n, reach),
        out_shape=jax.ShapeDtypeStruct((width, rows), BF),
        in_specs=[pl.BlockSpec(memory_space=pl.ANY)] * 13,
        out_specs=pl.BlockSpec(memory_space=pl.ANY),
        scratch_shapes=scratch,
        compiler_params=pltpu.CompilerParams(collective_id=0, has_side_effects=True),
        name="layer_backward",
    )(up, xin, inv, gain, q, k, v, ao, wq, wk, wv, wo, lens)
    return out.T[None]


def solution(mesh):
    placed = (
        P("pipe", "ctx", "tp"),
        P("pipe", "ctx", "tp"),
        P("pipe", "ctx"),
        P("pipe", "tp"),
        P("pipe", "ctx", "tp"),
        P("pipe", "ctx", "tp"),
        P("pipe", "ctx", "tp"),
        P("pipe", "ctx", "tp"),
        P("pipe", None, "tp"),
        P("pipe", None, "tp"),
        P("pipe", None, "tp"),
        P("pipe", "tp", None),
        P("pipe"),
    )
    return jax.shard_map(
        per_device, mesh=mesh, in_specs=placed, out_specs=P("pipe", "ctx", "tp"), check_vma=False
    )
```

```python
import functools

import jax
import jax.numpy as jnp
from jax import lax
from jax.experimental import pallas as pl
from jax.experimental.pallas import tpu as pltpu
from jax.sharding import PartitionSpec as P

QUERY_HEADS = 16
KEY_VALUE_HEADS = 8
HEAD_SIZE = 128
WINDOW = 1024
QUERY_SCALAR = 168
NEG_FILL = -1e30
GATHER_ROWS = 256
CHUNK_ROWS = 128
CHUNK_TAIL = 64
COUPLING_ROWS = 16
NT = (((1,), (1,)), ((), ()))
NN = (((1,), (0,)), ((), ()))
TN = (((0,), (0,)), ((), ()))
BF = jnp.bfloat16
F32 = jnp.float32


def chunk_cuts(width):
    cuts, at = [], 0
    while width - at > CHUNK_ROWS + CHUNK_TAIL // 2:
        cuts.append((at, CHUNK_ROWS))
        at += CHUNK_ROWS
    if width - at > CHUNK_TAIL:
        cuts.append((at, width - at - CHUNK_TAIL))
        at = width - CHUNK_TAIL
    return cuts + [(at, width - at)]


def gather_cuts(width):
    return [(at, min(GATHER_ROWS, width - at)) for at in range(0, width, GATHER_ROWS)]


def chunk_groups(chunks):
    groups, first, count = [], 0, 1
    while first < chunks:
        count = min(count, chunks - first)
        groups.append((first, count))
        first, count = first + count, count + 1
    return groups


def direct_reach(reach):
    return [d for d in range(1, reach + 1) if d != 2]


def far_reach(reach):
    return [d for d in direct_reach(reach) if reach >= 2]


def dot(a, b, dims):
    return lax.dot_general(a, b, dims, preferred_element_type=F32)


def kernel(
    ctx_n,
    pipe_n,
    reach,
    up_h,
    xin_h,
    inv_h,
    gain_h,
    q_h,
    k_h,
    v_h,
    ao_h,
    wq_h,
    wk_h,
    wv_h,
    wo_h,
    len_h,
    out_h,
    gath,
    xin,
    inv,
    gain,
    q,
    kb,
    vb,
    ao,
    wq,
    wk,
    wv,
    wo,
    slen,
    wo_cut,
    gain_col,
    ao_t,
    q_t,
    k_t,
    do_t,
    stat,
    s,
    dp,
    ds,
    q_far,
    do_far,
    stat_far,
    s_far,
    part_v,
    part_k,
    dq_low,
    snd,
    rcv,
    pacc,
    rs_a,
    rs_ar,
    rs_b,
    rs_br,
    rs_c,
    rs_cr,
    res,
    lsem,
    kv_s,
    k_r,
    v_r,
    ag_s,
    ag_r,
    q_s,
    q_r,
    do_s,
    do_r,
    st_s,
    st_r,
    acc_s,
    acc_r,
    from_low,
    from_high,
    rs_s,
    rs_rv,
    x_s,
    x_r,
):
    i = lax.axis_index("ctx")
    p = lax.axis_index("pipe")
    t = lax.axis_index("tp")
    partner = t + 1 - 2 * (t % 2)
    cross = (t + 2) % 4
    diag = 3 - t
    rows = q.shape[0]
    width = xin.shape[0]
    kv_heads = kb.shape[1] // HEAD_SIZE
    group = q.shape[1] // kb.shape[1]
    stacked = group * rows
    scale = QUERY_SCALAR ** (-0.5)
    model_width = width * 4
    chunk = chunk_cuts(width)
    chunks = len(chunk)
    cuts = gather_cuts(width)
    direct = direct_reach(reach)
    far = far_reach(reach)

    def local(src, dst, n):
        c = pltpu.make_async_copy(src, dst, lsem.at[n])
        c.start()
        return c

    def remote(src, dst, ss, rs, dev):
        return pltpu.make_async_remote_copy(
            src_ref=src,
            dst_ref=dst,
            send_sem=ss,
            recv_sem=rs,
            device_id=dev,
            device_id_type=pl.DeviceIdType.MESH,
        )

    barrier = pltpu.get_barrier_semaphore()

    def greet(dev):
        pl.semaphore_signal(
            barrier, inc=1, device_id=dev, device_id_type=pl.DeviceIdType.MESH
        )

    has_up = i + 1 < ctx_n
    has_down = i > 0

    greet({"tp": cross})
    greet({"tp": partner})
    expect = 2
    if reach >= 1:

        @pl.when(has_down)
        def _():
            greet({"ctx": i - 1})

        @pl.when(has_up)
        def _():
            greet({"ctx": i + 1})

        expect = expect + jnp.where(has_up, 1, 0) + jnp.where(has_down, 1, 0)
    prev = (p + pipe_n - 1) % pipe_n
    if pipe_n > 1:
        greet({"pipe": prev})
        expect += 1
    if pipe_n > 2:
        greet({"pipe": (p + 1) % pipe_n})
        expect += 1

    c_q = local(q_h, q, 1)
    c_k = local(k_h, kb.at[pl.ds(0, rows)], 0)
    c_len = local(len_h, slen, 2)
    c_up = local(up_h, gath.at[t], 3)
    c_wo = local(wo_h, wo, 5)
    c_ao = local(ao_h, ao, 6)
    c_gain = local(gain_h, gain, 12)
    c_v = local(v_h, vb.at[pl.ds(0, rows)], 4)
    c_wq = local(wq_h, wq, 7)
    c_wk = local(wk_h, wk, 8)
    c_wv = local(wv_h, wv, 9)
    c_xin = local(xin_h, xin, 10)
    c_inv = local(inv_h, inv, 11)

    def head_cols(h):
        return slice(h * HEAD_SIZE, (h + 1) * HEAD_SIZE)

    def block_rows(d):
        return slice(d * rows, (d + 1) * rows)

    def flip(x):
        return x.astype(F32).T

    pl.semaphore_wait(barrier, expect)

    def kv_copy(src_h, buf, ss, rs, d):
        dst = buf.at[pl.ds(d * rows, rows)]
        if d == 2:
            return remote(buf.at[pl.ds(rows, rows)], dst, ss.at[d - 1], rs.at[d - 1], {"ctx": i + 1})
        return remote(src_h, dst, ss.at[d - 1], rs.at[d - 1], {"ctx": i + d})

    def k_copy(d):
        return kv_copy(k_h, kb, kv_s, k_r, d)

    def v_copy(d):
        return kv_copy(v_h, vb, kv_s, v_r, d)

    def sends_up(d):
        return has_up & has_down if d == 2 else i + d < ctx_n

    def q_copy(n):
        return remote(q_t, q_far.at[n], q_s.at[n], q_r.at[n], {"ctx": i - far[n]})

    def do_copy(n, g):
        return remote(
            do_t.at[g], do_far.at[n, g], do_s.at[n], do_r.at[n, g], {"ctx": i - far[n]}
        )

    def stat_copy(n):
        return remote(stat, stat_far.at[n], st_s.at[n], st_r.at[n], {"ctx": i - far[n]})

    def sends_far(n):
        return i >= 2 if far[n] == 1 else i >= far[n]

    def takes_far(n):
        return has_up & has_down if far[n] == 1 else i + far[n] < ctx_n

    if reach >= 2:
        sends_acc = has_down & has_up
        takes_acc = i + 2 < ctx_n
    else:
        sends_acc = has_down
        takes_acc = has_up

    def acc_copy(g):
        return remote(snd.at[g], rcv.at[g], acc_s, acc_r.at[g], {"ctx": i - 1})

    parts = len(cuts)

    def ag_cross(n):
        sl = pl.ds(*cuts[n])
        return remote(up_h.at[sl], gath.at[t, sl], ag_s, ag_r.at[n], {"tp": cross})

    def ag_fwd(n):
        sl = pl.ds(*cuts[n])
        m = parts + n
        return remote(
            gath.at[cross, sl], gath.at[cross, sl], ag_s, ag_r.at[m], {"tp": partner}
        )

    ag_part = remote(
        up_h, gath.at[t], ag_s, ag_r.at[2 * parts], {"tp": partner}
    )
    def token(sem, cond, dev):
        @pl.when(cond)
        def _():
            pl.semaphore_signal(
                sem, inc=1, device_id=dev, device_id_type=pl.DeviceIdType.MESH
            )

    def relay(step):
        if step > 0:

            @pl.when(i >= step + 1)
            def _():
                pl.semaphore_wait(from_low, 1)

            @pl.when(i + step + 1 < ctx_n)
            def _():
                pl.semaphore_wait(from_high, 1)

        if step + 1 < reach:
            token(from_low, has_up & (i >= step + 1), {"ctx": i + 1})
            token(from_high, has_down & (i + step + 1 < ctx_n), {"ctx": i - 1})

    if reach >= 3:
        relay(0)
    for n in range(parts):
        ag_cross(n).start()
    if reach >= 1:

        @pl.when(has_up)
        def _():
            k_copy(1).start()
            v_copy(1).start()

    ag_part.start()
    c_q.wait()
    for g in range(kv_heads):
        for r in range(group):
            q_t[g, :, block_rows(r)] = flip(q[:, head_cols(g * group + r)]).astype(BF)

    if far:

        @pl.when(sends_far(0))
        def _():
            q_copy(0).start()


    for d in range(1, reach + 1):

        @pl.when(i < d)
        def _():
            kb[block_rows(d)] = jnp.zeros((rows, kb.shape[1]), BF)
            vb[block_rows(d)] = jnp.zeros((rows, vb.shape[1]), BF)

    c_len.wait()
    length = slen[0]
    key_i = lax.broadcasted_iota(jnp.int32, (rows, stacked), 0)
    qry_i = lax.broadcasted_iota(jnp.int32, (rows, stacked), 1) % rows
    later0 = qry_i - key_i
    pos_q = i * rows + qry_i
    live = (pos_q < length)[:1]

    def allowed(query_pos, d):
        later = later0 + d * rows
        pos_k = query_pos - later
        ok = (later >= 0) & (later < WINDOW) & (pos_k < length) & (query_pos < length)
        return ok & (pos_k >= 0)

    def scores(d):
        ok = allowed(pos_q, d)
        for g in range(kv_heads):
            keys = kb[block_rows(d), head_cols(g)]
            sc = dot(keys, q_t[g], NN) * scale
            s[g, block_rows(d)] = jnp.where(ok, sc, NEG_FILL)
            k_t[g, :, block_rows(d)] = flip(keys).astype(BF)

    c_k.wait()
    scores(0)
    c_wo.wait()
    for n in range(4):
        wo_cut[n] = wo[:, n * width : (n + 1) * width]
    c_ao.wait()
    for h in range(kv_heads * group):
        ao_t[head_cols(h), :] = flip(ao[:, head_cols(h)])
    c_gain.wait()
    gain_col[...] = jnp.broadcast_to(gain[...], (rows, width)).T
    if reach >= 3:
        relay(1)

    c_up.wait()
    acc = dot(wo_cut[t], gath[t], NN)
    ag_part.wait_recv()
    acc = acc + dot(wo_cut[partner], gath[partner], NN)

    for step in range(2, reach):
        relay(step)
    for d in direct[1:]:

        @pl.when(sends_up(d))
        def _():
            k_copy(d).start()

    for n in range(1, len(far)):

        @pl.when(sends_far(n))
        def _():
            q_copy(n).start()

    def take(copy, d):
        @pl.when(i >= d)
        def _():
            copy(d).wait_recv()

    def pass_on(copy):
        if reach >= 2:

            @pl.when(sends_up(2))
            def _():
                copy(2).start()

    if reach >= 1:
        take(k_copy, 1)
        pass_on(k_copy)
        scores(1)

    def shard_dot(owner, n):
        at, size = cuts[n]
        return dot(wo_cut[owner, :, at : at + size], gath[owner, at : at + size], NN)

    for n in range(parts):
        ag_cross(n).wait_recv()
        ag_fwd(n).start()
        acc = acc + shard_dot(cross, n)
        if n > 0:
            ag_fwd(n - 1).wait_recv()
            acc = acc + shard_dot(diag, n - 1)
    if reach >= 1:
        take(v_copy, 1)
        pass_on(v_copy)
    ag_fwd(parts - 1).wait_recv()
    acc = acc + shard_dot(diag, parts - 1)
    grad = acc.astype(BF)
    for g in range(kv_heads):
        for r in range(group):
            do_t[g, :, block_rows(r)] = grad[head_cols(g * group + r)]

    def send_dout(n, heads):
        @pl.when(sends_far(n))
        def _():
            for g in heads:
                do_copy(n, g).start()

    def send_stat(n):
        @pl.when(sends_far(n))
        def _():
            stat_copy(n).start()

    if far:
        send_dout(0, range(1))

    for g in range(kv_heads):
        sums = []
        for r in range(group):
            h = g * group + r
            sums.append(
                jnp.sum(
                    grad[head_cols(h)].astype(F32) * ao_t[head_cols(h), :], axis=0, keepdims=True
                )
            )
        stat[3 * g + 2 : 3 * g + 3, :] = jnp.concatenate(sums, axis=1)

    for d in range(2, reach + 1):
        take(k_copy, d)
        scores(d)

    for g in range(kv_heads):
        top = jnp.max(s[g], axis=0, keepdims=True)
        total = jnp.zeros((1, stacked), F32)
        for d in range(reach + 1):
            e = jnp.exp(s[g, block_rows(d)] - top)
            s[g, block_rows(d)] = e
            total = total + jnp.sum(e, axis=0, keepdims=True)
        inv_total = jnp.where(live, 1.0 / total, 0.0)
        for d in range(reach + 1):
            s[g, block_rows(d)] = s[g, block_rows(d)] * inv_total
        stat[3 * g : 3 * g + 1, :] = top
        stat[3 * g + 1 : 3 * g + 2, :] = inv_total

    if far:
        send_stat(0)
        for n in range(1, len(far)):
            send_dout(n, range(1))
            send_stat(n)
        for n in range(len(far)):
            send_dout(n, range(1, kv_heads))
    for d in direct[1:]:

        @pl.when(sends_up(d))
        def _():
            v_copy(d).start()

    c_v.wait()
    for d in range(2, reach + 1):
        take(v_copy, d)

    own = min(reach, 1) + 1
    for g in range(kv_heads):
        dp[g] = dot(vb[:, head_cols(g)], do_t[g], NN)
        part_v[g] = dot(s[g, : own * rows].astype(BF), do_t[g], NT)
        delta = stat[3 * g + 2 : 3 * g + 3, :]
        for d in range(reach + 1):
            ds[g, block_rows(d)] = (
                s[g, block_rows(d)] * (dp[g, block_rows(d)] - delta)
            ).astype(BF)
        part_k[g] = dot(ds[g, : own * rows], q_t[g], NT)

    def send_acc(g):
        snd[g, :rows] = part_v[g, block_rows(1)].astype(BF)
        snd[g, rows:] = part_k[g, block_rows(1)].astype(BF)
        acc_copy(g).start()

    if reach == 1:

        @pl.when(has_down)
        def _():
            for g in range(kv_heads):
                send_acc(g)

    if reach >= 2:

        @pl.when(i != 1)
        def _():
            part_v[:, block_rows(1)] = jnp.zeros((kv_heads, rows, HEAD_SIZE), F32)
            part_k[:, block_rows(1)] = jnp.zeros((kv_heads, rows, HEAD_SIZE), F32)

    coupling = jnp.zeros((1, rows), F32)
    low = []
    for g in range(kv_heads):
        dq = dot(k_t[g], ds[g], NN) * scale
        for r in range(group):
            part = dq[:, block_rows(r)].astype(BF)
            low.append(part)
            coupling = coupling + jnp.sum(
                part.astype(F32) * q_t[g, :, block_rows(r)].astype(F32), axis=0, keepdims=True
            )
    dq_low[...] = jnp.concatenate(low, axis=0)
    owners = (diag, cross, partner, t)

    def piece_rows(n, at=0, size=width):
        return pl.ds(pl.multiple_of(owners[n] * width + at, 16), size)

    def far_blocks(n):
        return ((1, 2), (0, 1)) if far[n] == 1 else ((0, far[n]),)

    def far_scores(n):
        @pl.when(takes_far(n))
        def _():
            q_copy(n).wait_recv()
            for at, (kd, dist) in enumerate(far_blocks(n)):
                ok = allowed((i + far[n]) * rows + qry_i, dist)
                for g in range(kv_heads):
                    sc = dot(kb[block_rows(kd), head_cols(g)], q_far[n, g], NN) * scale
                    s_far[n, g, block_rows(at)] = jnp.where(ok, sc, NEG_FILL)

    def far_pair(n):
        @pl.when(takes_far(n))
        def _():
            stat_copy(n).wait_recv()
            for at in range(len(far_blocks(n))):
                for g in range(kv_heads):
                    top = stat_far[n, 3 * g : 3 * g + 1, :]
                    inv_total = stat_far[n, 3 * g + 1 : 3 * g + 2, :]
                    s_far[n, g, block_rows(at)] = (
                        jnp.exp(s_far[n, g, block_rows(at)] - top) * inv_total
                    )
            for g in range(kv_heads):
                delta = stat_far[n, 3 * g + 2 : 3 * g + 3, :]
                do_copy(n, g).wait_recv()
                for at, (kd, _) in enumerate(far_blocks(n)):
                    pr = s_far[n, g, block_rows(at)]
                    part_v[g, block_rows(kd)] += dot(pr.astype(BF), do_far[n, g], NT)
                    dprob = dot(vb[block_rows(kd), head_cols(g)], do_far[n, g], NN)
                    dsc = (pr * (dprob - delta)).astype(BF)
                    part_k[g, block_rows(kd)] += dot(dsc, q_far[n, g], NT)
                    if kd == 1:
                        send_acc(g)

    def project_query():
        c_wq.wait()
        for n in range(4):
            pacc[n] = dot(wq[piece_rows(n), :], dq_low[...], NN)

    if far:
        early = i < 2
        far_scores(0)
        pl.when(early)(project_query)
        far_pair(0)
        pl.when(jnp.logical_not(early))(project_query)
    else:
        project_query()
    for n in range(1, len(far)):
        far_scores(n)
    for n in range(1, len(far)):
        far_pair(n)
    c_wk.wait()
    c_wv.wait()
    c_xin.wait()
    c_inv.wait()
    if reach >= 1:

        @pl.when(takes_acc)
        def _():
            for g in range(kv_heads):
                acc_copy(g).wait_recv()
                part_v[g, :rows] += rcv[g, :rows].astype(F32)
                part_k[g, :rows] += rcv[g, rows:].astype(F32)

    dv_low = jnp.concatenate([part_v[g, :rows].astype(BF) for g in range(kv_heads)], axis=1)
    dk_low = jnp.concatenate(
        [(part_k[g, :rows] * scale).astype(BF) for g in range(kv_heads)], axis=1
    )
    both = dk_low.astype(F32) * kb[:rows].astype(F32) + dv_low.astype(F32) * vb[:rows].astype(F32)
    for g in range(kv_heads):
        coupling = coupling + jnp.sum(both[:, head_cols(g)].T, axis=0, keepdims=True)

    def piece(n, at=0, size=width):
        span = piece_rows(n, at, size)
        more = dot(wk[span, :], dk_low, NT) + dot(wv[span, :], dv_low, NT)
        return pacc[n, at : at + size] + more

    lead = COUPLING_ROWS
    wide = jnp.broadcast_to(coupling, (lead, rows))

    def span_of(first, count=1):
        at, size = chunk[first][0], sum(chunk[n][1] for n in range(first, first + count))
        return (0, lead + size) if first == 0 else (lead + at, size)

    groups = chunk_groups(chunks)

    def a_copy(m):
        sl = pl.ds(*span_of(*groups[m]))
        return remote(rs_a.at[sl], rs_ar.at[sl], rs_s.at[0], rs_rv.at[1 + m], {"tp": partner})

    send_c = remote(rs_c, rs_cr, rs_s.at[1], rs_rv.at[0], {"tp": partner})
    base = 1 + len(groups)

    def b_copy(n):
        sl = pl.ds(*span_of(n))
        return remote(rs_b.at[sl], rs_br.at[sl], rs_s.at[2], rs_rv.at[base + n], {"tp": cross})

    def x_copy(at, size):
        sl = pl.ds(at, size)
        if pipe_n == 1:
            return pltpu.make_async_copy(res.at[sl], out_h.at[sl], x_s)
        return remote(res.at[sl], out_h.at[sl], x_s, x_r, {"pipe": prev})

    rs_a[:lead, :] = wide.astype(BF)
    for m, (first, count) in enumerate(groups):
        at, size = chunk[first][0], sum(chunk[n][1] for n in range(first, first + count))
        rs_a[lead + at : lead + at + size, :] = piece(0, at, size).astype(BF)
        a_copy(m).start()
    for m, (first, count) in enumerate(groups):
        at, size = chunk[first][0], sum(chunk[n][1] for n in range(first, first + count))
        pacc[1, at : at + size] = piece(1, at, size)
        a_copy(m).wait_recv()
        if m == 0:
            rs_b[:lead, :] = (wide + rs_ar[:lead, :].astype(F32)).astype(BF)
        for n in range(first, first + count):
            at, size = chunk[n]
            sl = slice(at, at + size)
            sh = slice(lead + at, lead + at + size)
            rs_b[sh, :] = (pacc[1, sl] + rs_ar[sh, :].astype(F32)).astype(BF)
            b_copy(n).start()
    rs_c[lead:, :] = piece(2).astype(BF)
    rs_c[:lead, :] = wide.astype(BF)
    send_c.start()
    pacc[3] = piece(3)
    iv = inv[...]
    send_c.wait_recv()
    for n in range(chunks):
        at, size = chunk[n]
        sl = slice(at, at + size)
        sh = slice(lead + at, lead + at + size)
        b_copy(n).wait_recv()
        if n == 0:
            coup = (
                coupling + rs_cr[:lead, :].astype(F32)[:1] + rs_br[:lead, :].astype(F32)[:1]
            )
            drag = iv * coup / model_width
        normed = pacc[3, sl] + rs_cr[sh, :].astype(F32) + rs_br[sh, :].astype(F32)
        val = gath[t, sl, :].astype(F32) + iv * (
            gain_col[sl, :] * normed - xin[sl, :].astype(F32) * drag
        )
        res[sl, :] = val.astype(BF)
        x_copy(at, size).start()

    shards = gath.at[pl.ds(0, 3)]
    remote(shards, shards, ag_s, ag_r.at[0], {"tp": partner}).wait_send()
    for d in range(1, reach + 1):

        @pl.when(sends_up(d))
        def _():
            both_blocks = kb.at[pl.ds(0, 2 * rows)]
            remote(
                both_blocks, both_blocks, kv_s.at[d - 1], k_r.at[d - 1], {"ctx": i + 1}
            ).wait_send()

    for n in range(len(far)):

        @pl.when(sends_far(n))
        def _():
            q_copy(n).wait_send()
            stat_copy(n).wait_send()
            remote(
                do_t, do_far.at[n], do_s.at[n], do_r.at[n, 0], {"ctx": i - far[n]}
            ).wait_send()

    if reach >= 1:

        @pl.when(sends_acc)
        def _():
            remote(snd, rcv, acc_s, acc_r.at[0], {"ctx": i - 1}).wait_send()

    send_c.wait_send()
    remote(rs_a, rs_ar, rs_s.at[0], rs_rv.at[1], {"tp": partner}).wait_send()
    remote(rs_b, rs_br, rs_s.at[2], rs_rv.at[base], {"tp": cross}).wait_send()
    x_copy(0, width).wait()


def per_device(up, xin, inv, gain, q, k, v, ao, wq, wk, wv, wo, lens):
    ctx_n = lax.axis_size("ctx")
    pipe_n = lax.axis_size("pipe")
    tp_n = lax.axis_size("tp")
    assert tp_n == 4
    up, xin, q, k, v, ao = up[0].T, xin[0].T, q[0], k[0], v[0], ao[0]
    wq, wk, wv, wo = wq[0], wk[0], wv[0], wo[0]
    width, rows = up.shape
    reach = min((WINDOW - 2 + rows) // rows, ctx_n - 1)
    kv_cols, q_cols = k.shape[1], q.shape[1]
    kv_heads = kv_cols // HEAD_SIZE
    stacked = rows * (q_cols // kv_cols)
    chunks = len(chunk_cuts(width))
    groups = len(chunk_groups(chunks))
    parts = len(gather_cuts(width))
    vm = pltpu.VMEM
    dma = pltpu.SemaphoreType.DMA
    blocks = reach + 1
    own = min(reach, 1) + 1
    far = max(len(far_reach(reach)), 1)
    stats = -(-3 * kv_heads // 8) * 8
    scratch = [
        vm((tp_n, width, rows), BF),
        vm((width, rows), BF),
        vm(inv.shape, F32),
        vm(gain.shape, F32),
        vm(q.shape, BF),
        vm((blocks * rows, kv_cols), BF),
        vm((blocks * rows, kv_cols), BF),
        vm(ao.shape, BF),
        vm(wq.shape, BF),
        vm(wk.shape, BF),
        vm(wv.shape, BF),
        vm(wo.shape, BF),
        pltpu.SMEM(lens.shape, jnp.int32),
        vm((tp_n, wo.shape[0], width), BF),
        vm((width, rows), F32),
        vm((q_cols, rows), F32),
        vm((kv_heads, HEAD_SIZE, stacked), BF),
        vm((kv_heads, HEAD_SIZE, blocks * rows), BF),
        vm((kv_heads, HEAD_SIZE, stacked), BF),
        vm((stats, stacked), F32),
        vm((kv_heads, blocks * rows, stacked), F32),
        vm((kv_heads, blocks * rows, stacked), F32),
        vm((kv_heads, blocks * rows, stacked), BF),
        vm((far, kv_heads, HEAD_SIZE, stacked), BF),
        vm((far, kv_heads, HEAD_SIZE, stacked), BF),
        vm((far, stats, stacked), F32),
        vm((far, kv_heads, 2 * rows, stacked), F32),
        vm((kv_heads, own * rows, HEAD_SIZE), F32),
        vm((kv_heads, own * rows, HEAD_SIZE), F32),
        vm((q_cols, rows), BF),
        vm((kv_heads, 2 * rows, HEAD_SIZE), BF),
        vm((kv_heads, 2 * rows, HEAD_SIZE), BF),
        vm((tp_n, width, rows), F32),
    ]
    scratch += [vm((COUPLING_ROWS + width, rows), BF)] * 6
    scratch += [vm((width, rows), BF)]
    scratch += [dma((13,))]
    scratch += [dma((max(reach, 1),))] * 3
    scratch += [dma(())]
    scratch += [dma((2 * parts + 1,))]
    scratch += [dma((far,))] * 2
    scratch += [dma((far,))]
    scratch += [dma((far, kv_heads))]
    scratch += [dma((far,))] * 2
    scratch += [dma(())]
    scratch += [dma((kv_heads,))]
    scratch += [pltpu.SemaphoreType.REGULAR] * 2
    scratch += [dma((3,))]
    scratch += [dma((1 + groups + chunks,))]
    scratch += [dma(())] * 2
    out = pl.pallas_call(
        functools.partial(kernel, ctx_n, pipe_n, reach),
        out_shape=vm((width, rows), BF),
        in_specs=[pl.BlockSpec(memory_space=pl.ANY)] * 13,
        out_specs=pl.BlockSpec(memory_space=vm),
        scratch_shapes=scratch,
        compiler_params=pltpu.CompilerParams(collective_id=0, has_side_effects=True),
        name="layer_backward",
    )(up, xin, inv, gain, q, k, v, ao, wq, wk, wv, wo, lens)
    return out.T[None]


def solution(mesh):
    placed = (
        P("pipe", "ctx", "tp"),
        P("pipe", "ctx", "tp"),
        P("pipe", "ctx"),
        P("pipe", "tp"),
        P("pipe", "ctx", "tp"),
        P("pipe", "ctx", "tp"),
        P("pipe", "ctx", "tp"),
        P("pipe", "ctx", "tp"),
        P("pipe", None, "tp"),
        P("pipe", None, "tp"),
        P("pipe", None, "tp"),
        P("pipe", "tp", None),
        P("pipe"),
    )
    return jax.shard_map(
        per_device, mesh=mesh, in_specs=placed, out_specs=P("pipe", "ctx", "tp"), check_vma=False
    )
```

```python
import functools

import jax
import jax.numpy as jnp
from jax import lax
from jax.experimental import pallas as pl
from jax.experimental.pallas import tpu as pltpu
from jax.sharding import PartitionSpec as P

QUERY_HEADS = 16
KEY_VALUE_HEADS = 8
HEAD_SIZE = 128
WINDOW = 1024
QUERY_SCALAR = 168
NEG_FILL = -1e30
GATHER_ROWS = 256
CHUNK_ROWS = 64
COUPLING_ROWS = 16
NT = (((1,), (1,)), ((), ()))
NN = (((1,), (0,)), ((), ()))
TN = (((0,), (0,)), ((), ()))
BF = jnp.bfloat16
F32 = jnp.float32


def chunk_cuts(width):
    return [(at, min(CHUNK_ROWS, width - at)) for at in range(0, width, CHUNK_ROWS)]


def gather_cuts(width):
    return [(at, min(GATHER_ROWS, width - at)) for at in range(0, width, GATHER_ROWS)]


def chunk_groups(chunks):
    edges = sorted({0, min(1, chunks), min(4, chunks), chunks})
    return [(a, b - a) for a, b in zip(edges, edges[1:])]


def direct_reach(reach):
    return [d for d in range(1, reach + 1) if d != 2]


def far_reach(reach):
    return [d for d in direct_reach(reach) if reach >= 2]


def dot(a, b, dims):
    return lax.dot_general(a, b, dims, preferred_element_type=F32)


def kernel(
    ctx_n,
    pipe_n,
    reach,
    up_h,
    xin_h,
    inv_h,
    gain_h,
    q_h,
    k_h,
    v_h,
    ao_h,
    wq_h,
    wk_h,
    wv_h,
    wo_h,
    len_h,
    out_h,
    gath,
    xin,
    inv,
    gain,
    q,
    kb,
    vb,
    ao,
    wq,
    wkv,
    wo,
    slen,
    wo_cut,
    gain_col,
    ao_t,
    q_t,
    k_t,
    do_t,
    stat,
    s,
    dp,
    ds,
    q_far,
    do_far,
    stat_far,
    s_far,
    part_v,
    part_k,
    dq_low,
    dkv,
    v_t,
    snd,
    rcv,
    pacc,
    rs_a,
    rs_ar,
    rs_b,
    rs_br,
    rs_c,
    rs_cr,
    res,
    lsem,
    kv_s,
    k_r,
    v_r,
    ag_s,
    ag_r,
    q_s,
    q_r,
    do_s,
    do_r,
    st_s,
    st_r,
    acc_s,
    acc_r,
    from_low,
    from_high,
    rs_s,
    rs_rv,
    x_s,
    x_r,
):
    i = lax.axis_index("ctx")
    p = lax.axis_index("pipe")
    t = lax.axis_index("tp")
    partner = t + 1 - 2 * (t % 2)
    cross = (t + 2) % 4
    diag = 3 - t
    rows = q.shape[0]
    width = xin.shape[0]
    kv_cols = kb.shape[1]
    kv_heads = kv_cols // HEAD_SIZE
    group = q.shape[1] // kb.shape[1]
    stacked = group * rows
    scale = QUERY_SCALAR ** (-0.5)
    model_width = width * 4
    chunk = chunk_cuts(width)
    chunks = len(chunk)
    cuts = gather_cuts(width)
    direct = direct_reach(reach)
    far = far_reach(reach)

    def local(src, dst, n):
        c = pltpu.make_async_copy(src, dst, lsem.at[n])
        c.start()
        return c

    def remote(src, dst, ss, rs, dev):
        return pltpu.make_async_remote_copy(
            src_ref=src,
            dst_ref=dst,
            send_sem=ss,
            recv_sem=rs,
            device_id=dev,
            device_id_type=pl.DeviceIdType.MESH,
        )

    barrier = pltpu.get_barrier_semaphore()

    def greet(dev):
        pl.semaphore_signal(
            barrier, inc=1, device_id=dev, device_id_type=pl.DeviceIdType.MESH
        )

    has_up = i + 1 < ctx_n
    has_down = i > 0

    greet({"tp": cross})
    greet({"tp": partner})
    expect = 2
    if reach >= 1:

        @pl.when(has_down)
        def _():
            greet({"ctx": i - 1})

        @pl.when(has_up)
        def _():
            greet({"ctx": i + 1})

        expect = expect + jnp.where(has_up, 1, 0) + jnp.where(has_down, 1, 0)
    prev = (p + pipe_n - 1) % pipe_n
    if pipe_n > 1:
        greet({"pipe": prev})
        expect += 1
    if pipe_n > 2:
        greet({"pipe": (p + 1) % pipe_n})
        expect += 1

    c_q = local(q_h, q, 1)
    c_k = local(k_h, kb.at[pl.ds(0, rows)], 0)
    c_len = local(len_h, slen, 2)
    c_up = local(up_h, gath.at[t], 3)
    c_wo = local(wo_h, wo, 5)
    c_ao = local(ao_h, ao, 6)
    c_gain = local(gain_h, gain, 12)
    c_v = local(v_h, vb.at[pl.ds(0, rows)], 4)
    c_wq = local(wq_h, wq, 7)
    c_wk = local(wk_h, wkv.at[:, pl.ds(0, kv_cols)], 8)
    c_wv = local(wv_h, wkv.at[:, pl.ds(kv_cols, kv_cols)], 9)
    c_xin = local(xin_h, xin, 10)
    c_inv = local(inv_h, inv, 11)

    def head_cols(h):
        return slice(h * HEAD_SIZE, (h + 1) * HEAD_SIZE)

    def block_rows(d):
        return slice(d * rows, (d + 1) * rows)

    def flip(x):
        return x.astype(F32).T

    pl.semaphore_wait(barrier, expect)

    def kv_copy(src_h, buf, ss, rs, d):
        dst = buf.at[pl.ds(d * rows, rows)]
        if d == 2:
            return remote(buf.at[pl.ds(rows, rows)], dst, ss.at[d - 1], rs.at[d - 1], {"ctx": i + 1})
        return remote(src_h, dst, ss.at[d - 1], rs.at[d - 1], {"ctx": i + d})

    def k_copy(d):
        return kv_copy(k_h, kb, kv_s, k_r, d)

    def v_copy(d):
        return kv_copy(v_h, vb, kv_s, v_r, d)

    def sends_up(d):
        return has_up & has_down if d == 2 else i + d < ctx_n

    def q_copy(n):
        return remote(q_t, q_far.at[n], q_s.at[n], q_r.at[n], {"ctx": i - far[n]})

    def do_copy(n, g):
        return remote(
            do_t.at[g], do_far.at[n, g], do_s.at[n], do_r.at[n, g], {"ctx": i - far[n]}
        )

    def stat_copy(n):
        return remote(stat, stat_far.at[n], st_s.at[n], st_r.at[n], {"ctx": i - far[n]})

    def sends_far(n):
        return i >= 2 if far[n] == 1 else i >= far[n]

    def takes_far(n):
        return has_up & has_down if far[n] == 1 else i + far[n] < ctx_n

    if reach >= 2:
        sends_acc = has_down & has_up
        takes_acc = i + 2 < ctx_n
    else:
        sends_acc = has_down
        takes_acc = has_up

    def acc_copy(g):
        return remote(snd.at[g], rcv.at[g], acc_s, acc_r.at[g], {"ctx": i - 1})

    parts = len(cuts)

    def ag_cross(n):
        sl = pl.ds(*cuts[n])
        return remote(up_h.at[sl], gath.at[t, sl], ag_s, ag_r.at[n], {"tp": cross})

    def ag_fwd(n):
        sl = pl.ds(*cuts[n])
        m = parts + n
        return remote(
            gath.at[cross, sl], gath.at[cross, sl], ag_s, ag_r.at[m], {"tp": partner}
        )

    last = pl.ds(*cuts[-1])
    ag_twin = remote(
        up_h.at[last], gath.at[t, last], ag_s, ag_r.at[2 * parts - 1], {"tp": diag}
    )
    ag_part = remote(
        up_h, gath.at[t], ag_s, ag_r.at[2 * parts], {"tp": partner}
    )
    def token(sem, cond, dev):
        @pl.when(cond)
        def _():
            pl.semaphore_signal(
                sem, inc=1, device_id=dev, device_id_type=pl.DeviceIdType.MESH
            )

    def relay(step):
        if step > 0:

            @pl.when(i >= step + 1)
            def _():
                pl.semaphore_wait(from_low, 1)

            @pl.when(i + step + 1 < ctx_n)
            def _():
                pl.semaphore_wait(from_high, 1)

        if step + 1 < reach:
            token(from_low, has_up & (i >= step + 1), {"ctx": i + 1})
            token(from_high, has_down & (i + step + 1 < ctx_n), {"ctx": i - 1})

    if reach >= 3:
        relay(0)
    for n in range(parts):
        ag_cross(n).start()
    first_core = t % 2 == 0
    if reach >= 1:

        @pl.when(has_up)
        def _():
            k_copy(1).start()
            v_copy(1).start()

    ag_part.start()
    c_q.wait()
    for g in range(kv_heads):
        for r in range(group):
            q_t[g, :, block_rows(r)] = flip(q[:, head_cols(g * group + r)]).astype(BF)

    if far:

        @pl.when(sends_far(0))
        def _():
            q_copy(0).start()


    for d in range(1, reach + 1):

        @pl.when(i < d)
        def _():
            kb[block_rows(d)] = jnp.zeros((rows, kb.shape[1]), BF)
            vb[block_rows(d)] = jnp.zeros((rows, vb.shape[1]), BF)

    c_len.wait()
    length = slen[0]
    key_i = lax.broadcasted_iota(jnp.int32, (rows, stacked), 0)
    qry_i = lax.broadcasted_iota(jnp.int32, (rows, stacked), 1) % rows
    later0 = qry_i - key_i
    pos_q = i * rows + qry_i
    live = (pos_q < length)[:1]

    def allowed(query_pos, d):
        later = later0 + d * rows
        pos_k = query_pos - later
        ok = (later >= 0) & (later < WINDOW) & (pos_k < length) & (query_pos < length)
        return ok & (pos_k >= 0)

    def scores(d):
        ok = allowed(pos_q, d)
        for g in range(kv_heads):
            keys = kb[block_rows(d), head_cols(g)]
            sc = dot(keys, q_t[g], NN) * scale
            s[g, block_rows(d)] = jnp.where(ok, sc, NEG_FILL)
            k_t[g, :, block_rows(d)] = flip(keys).astype(BF)

    c_k.wait()
    scores(0)
    c_wo.wait()
    for n in range(4):
        wo_cut[n] = wo[:, n * width : (n + 1) * width]
    c_ao.wait()
    for h in range(kv_heads * group):
        ao_t[head_cols(h), :] = flip(ao[:, head_cols(h)])
    c_v.wait()
    for g in range(kv_heads):
        v_t[g] = flip(vb[:rows, head_cols(g)])
    c_gain.wait()
    gain_col[...] = jnp.broadcast_to(gain[...], (rows, width)).T
    if reach >= 3:
        relay(1)

    def shard_dot(owner, n):
        at, size = cuts[n]
        return dot(wo_cut[owner, :, at : at + size], gath[owner, at : at + size], NN)

    c_up.wait()
    acc = dot(wo_cut[t], gath[t], NN)
    ag_part.wait_recv()

    @pl.when(first_core)
    def _():
        ag_twin.start()

    acc = acc + dot(wo_cut[partner], gath[partner], NN)

    for step in range(2, reach):
        relay(step)
    for d in direct[1:]:

        @pl.when(sends_up(d))
        def _():
            k_copy(d).start()

    for n in range(1, len(far)):

        @pl.when(sends_far(n))
        def _():
            q_copy(n).start()

    def take(copy, d):
        @pl.when(i >= d)
        def _():
            copy(d).wait_recv()

    def pass_on(copy):
        if reach >= 2:

            @pl.when(sends_up(2))
            def _():
                copy(2).start()

    if reach >= 1:
        take(k_copy, 1)
        pass_on(k_copy)
        scores(1)

    for n in range(parts):
        ag_cross(n).wait_recv()
        if n + 1 < parts:
            ag_fwd(n).start()
        else:
            pl.when(jnp.logical_not(first_core))(ag_fwd(n).start)
        acc = acc + shard_dot(cross, n)
    for n in range(parts):
        if n + 1 == parts and reach >= 1:
            take(v_copy, 1)
            pass_on(v_copy)
        ag_fwd(n).wait_recv()
        acc = acc + shard_dot(diag, n)
    grad = acc.astype(BF)
    for g in range(kv_heads):
        for r in range(group):
            do_t[g, :, block_rows(r)] = grad[head_cols(g * group + r)]

    def send_dout(n, heads):
        @pl.when(sends_far(n))
        def _():
            for g in heads:
                do_copy(n, g).start()

    def send_stat(n):
        @pl.when(sends_far(n))
        def _():
            stat_copy(n).start()

    if far:
        send_dout(0, range(1))

    for g in range(kv_heads):
        sums = []
        for r in range(group):
            h = g * group + r
            sums.append(
                jnp.sum(
                    grad[head_cols(h)].astype(F32) * ao_t[head_cols(h), :], axis=0, keepdims=True
                )
            )
        stat[3 * g + 2 : 3 * g + 3, :] = jnp.concatenate(sums, axis=1)

    for d in range(2, reach + 1):
        take(k_copy, d)
        scores(d)

    for g in range(kv_heads):
        top = jnp.max(s[g], axis=0, keepdims=True)
        total = jnp.zeros((1, stacked), F32)
        for d in range(reach + 1):
            e = jnp.exp(s[g, block_rows(d)] - top)
            s[g, block_rows(d)] = e
            total = total + jnp.sum(e, axis=0, keepdims=True)
        inv_total = jnp.where(live, 1.0 / total, 0.0)
        for d in range(reach + 1):
            s[g, block_rows(d)] = s[g, block_rows(d)] * inv_total
        stat[3 * g : 3 * g + 1, :] = top
        stat[3 * g + 1 : 3 * g + 2, :] = inv_total

    if far:
        send_stat(0)
        for n in range(1, len(far)):
            send_dout(n, range(1))
            send_stat(n)
        for n in range(len(far)):
            send_dout(n, range(1, kv_heads))
    for d in direct[1:]:

        @pl.when(sends_up(d))
        def _():
            v_copy(d).start()

    for d in range(2, reach + 1):
        take(v_copy, d)

    own = min(reach, 1) + 1
    for g in range(kv_heads):
        dp[g] = dot(vb[:, head_cols(g)], do_t[g], NN)
        part_v[g] = dot(do_t[g], s[g, : own * rows].astype(BF), NT)
        delta = stat[3 * g + 2 : 3 * g + 3, :]
        for d in range(reach + 1):
            ds[g, block_rows(d)] = (
                s[g, block_rows(d)] * (dp[g, block_rows(d)] - delta)
            ).astype(BF)
        part_k[g] = dot(q_t[g], ds[g, : own * rows], NT)

    def send_acc(g):
        snd[g, :HEAD_SIZE] = part_v[g, :, block_rows(1)].astype(BF)
        snd[g, HEAD_SIZE:] = part_k[g, :, block_rows(1)].astype(BF)
        acc_copy(g).start()

    if reach == 1:

        @pl.when(has_down)
        def _():
            for g in range(kv_heads):
                send_acc(g)

    if reach >= 2:

        @pl.when(i != 1)
        def _():
            part_v[:, :, block_rows(1)] = jnp.zeros((kv_heads, HEAD_SIZE, rows), F32)
            part_k[:, :, block_rows(1)] = jnp.zeros((kv_heads, HEAD_SIZE, rows), F32)

    coupling = jnp.zeros((1, rows), F32)
    low = []
    for g in range(kv_heads):
        dq = dot(k_t[g], ds[g], NN) * scale
        for r in range(group):
            part = dq[:, block_rows(r)].astype(BF)
            low.append(part)
            coupling = coupling + jnp.sum(
                part.astype(F32) * q_t[g, :, block_rows(r)].astype(F32), axis=0, keepdims=True
            )
    dq_low[...] = jnp.concatenate(low, axis=0)
    owners = (diag, cross, partner, t)

    def piece_rows(n, at=0, size=width):
        return pl.ds(pl.multiple_of(owners[n] * width + at, 16), size)

    def far_blocks(n):
        return ((1, 2), (0, 1)) if far[n] == 1 else ((0, far[n]),)

    def far_scores(n):
        @pl.when(takes_far(n))
        def _():
            q_copy(n).wait_recv()
            for at, (kd, dist) in enumerate(far_blocks(n)):
                ok = allowed((i + far[n]) * rows + qry_i, dist)
                for g in range(kv_heads):
                    sc = dot(kb[block_rows(kd), head_cols(g)], q_far[n, g], NN) * scale
                    s_far[n, g, block_rows(at)] = jnp.where(ok, sc, NEG_FILL)

    def far_pair(n):
        @pl.when(takes_far(n))
        def _():
            stat_copy(n).wait_recv()
            for at in range(len(far_blocks(n))):
                for g in range(kv_heads):
                    top = stat_far[n, 3 * g : 3 * g + 1, :]
                    inv_total = stat_far[n, 3 * g + 1 : 3 * g + 2, :]
                    s_far[n, g, block_rows(at)] = (
                        jnp.exp(s_far[n, g, block_rows(at)] - top) * inv_total
                    )
            for g in range(kv_heads):
                delta = stat_far[n, 3 * g + 2 : 3 * g + 3, :]
                do_copy(n, g).wait_recv()
                for at, (kd, _) in enumerate(far_blocks(n)):
                    pr = s_far[n, g, block_rows(at)]
                    part_v[g, :, block_rows(kd)] += dot(do_far[n, g], pr.astype(BF), NT)
                    dprob = dot(vb[block_rows(kd), head_cols(g)], do_far[n, g], NN)
                    dsc = (pr * (dprob - delta)).astype(BF)
                    part_k[g, :, block_rows(kd)] += dot(q_far[n, g], dsc, NT)
                    if kd == 1:
                        send_acc(g)

    def project_query():
        c_wq.wait()
        for n in range(4):
            pacc[n] = dot(wq[piece_rows(n), :], dq_low[...], NN)

    if far:
        early = i < 2
        far_scores(0)
        pl.when(early)(project_query)
        far_pair(0)
        pl.when(jnp.logical_not(early))(project_query)
    else:
        project_query()
    for n in range(1, len(far)):
        far_scores(n)
    for n in range(1, len(far)):
        far_pair(n)
    c_wk.wait()
    c_wv.wait()
    c_xin.wait()
    c_inv.wait()
    if reach >= 1:

        @pl.when(takes_acc)
        def _():
            for g in range(kv_heads):
                acc_copy(g).wait_recv()
                part_v[g, :, :rows] += rcv[g, :HEAD_SIZE].astype(F32)
                part_k[g, :, :rows] += rcv[g, HEAD_SIZE:].astype(F32)

    for g in range(kv_heads):
        dk_low = (part_k[g, :, :rows] * scale).astype(BF)
        dv_low = part_v[g, :, :rows].astype(BF)
        dkv[head_cols(g), :] = dk_low
        dkv[head_cols(kv_heads + g), :] = dv_low
        both = dk_low.astype(F32) * k_t[g, :, :rows].astype(F32) + dv_low.astype(F32) * v_t[g]
        coupling = coupling + jnp.sum(both, axis=0, keepdims=True)

    def piece(n, at=0, size=width):
        return pacc[n, at : at + size] + dot(wkv[piece_rows(n, at, size), :], dkv[...], NN)

    lead = COUPLING_ROWS
    wide = jnp.broadcast_to(coupling, (lead, rows))

    def span_of(first, count=1):
        at, size = chunk[first][0], sum(chunk[n][1] for n in range(first, first + count))
        return (0, lead + size) if first == 0 else (lead + at, size)

    groups = chunk_groups(chunks)

    def a_copy(m):
        sl = pl.ds(*span_of(*groups[m]))
        return remote(rs_a.at[sl], rs_ar.at[sl], rs_s.at[0], rs_rv.at[1 + m], {"tp": partner})

    send_c = remote(rs_c, rs_cr, rs_s.at[1], rs_rv.at[0], {"tp": partner})
    base = 1 + len(groups)

    def b_copy(n):
        sl = pl.ds(*span_of(n))
        return remote(rs_b.at[sl], rs_br.at[sl], rs_s.at[2], rs_rv.at[base + n], {"tp": cross})

    def x_copy(at, size):
        sl = pl.ds(at, size)
        if pipe_n == 1:
            return pltpu.make_async_copy(res.at[sl], out_h.at[sl], x_s)
        return remote(res.at[sl], out_h.at[sl], x_s, x_r, {"pipe": prev})

    rs_a[:lead, :] = wide.astype(BF)
    for m, (first, count) in enumerate(groups):
        at, size = chunk[first][0], sum(chunk[n][1] for n in range(first, first + count))
        rs_a[lead + at : lead + at + size, :] = piece(0, at, size).astype(BF)
        a_copy(m).start()
    for m, (first, count) in enumerate(groups):
        at, size = chunk[first][0], sum(chunk[n][1] for n in range(first, first + count))
        pacc[1, at : at + size] = piece(1, at, size)
        a_copy(m).wait_recv()
        if m == 0:
            rs_b[:lead, :] = (wide + rs_ar[:lead, :].astype(F32)).astype(BF)
        for n in range(first, first + count):
            at, size = chunk[n]
            sl = slice(at, at + size)
            sh = slice(lead + at, lead + at + size)
            rs_b[sh, :] = (pacc[1, sl] + rs_ar[sh, :].astype(F32)).astype(BF)
            b_copy(n).start()
    rs_c[lead:, :] = piece(2).astype(BF)
    rs_c[:lead, :] = wide.astype(BF)
    send_c.start()
    pacc[3] = piece(3)
    iv = inv[...]
    send_c.wait_recv()
    for n in range(chunks):
        at, size = chunk[n]
        sl = slice(at, at + size)
        sh = slice(lead + at, lead + at + size)
        b_copy(n).wait_recv()
        if n == 0:
            coup = (
                coupling + rs_cr[:lead, :].astype(F32)[:1] + rs_br[:lead, :].astype(F32)[:1]
            )
            drag = iv * coup / model_width
        normed = pacc[3, sl] + rs_cr[sh, :].astype(F32) + rs_br[sh, :].astype(F32)
        val = gath[t, sl, :].astype(F32) + iv * (
            gain_col[sl, :] * normed - xin[sl, :].astype(F32) * drag
        )
        res[sl, :] = val.astype(BF)
        x_copy(at, size).start()

    shards = gath.at[pl.ds(0, 3)]
    remote(shards, shards, ag_s, ag_r.at[0], {"tp": partner}).wait_send()
    for d in range(1, reach + 1):

        @pl.when(sends_up(d))
        def _():
            both_blocks = kb.at[pl.ds(0, 2 * rows)]
            remote(
                both_blocks, both_blocks, kv_s.at[d - 1], k_r.at[d - 1], {"ctx": i + 1}
            ).wait_send()

    for n in range(len(far)):

        @pl.when(sends_far(n))
        def _():
            q_copy(n).wait_send()
            stat_copy(n).wait_send()
            remote(
                do_t, do_far.at[n], do_s.at[n], do_r.at[n, 0], {"ctx": i - far[n]}
            ).wait_send()

    if reach >= 1:

        @pl.when(sends_acc)
        def _():
            remote(snd, rcv, acc_s, acc_r.at[0], {"ctx": i - 1}).wait_send()

    send_c.wait_send()
    remote(rs_a, rs_ar, rs_s.at[0], rs_rv.at[1], {"tp": partner}).wait_send()
    remote(rs_b, rs_br, rs_s.at[2], rs_rv.at[base], {"tp": cross}).wait_send()
    x_copy(0, width).wait()


def per_device(up, xin, inv, gain, q, k, v, ao, wq, wk, wv, wo, lens):
    ctx_n = lax.axis_size("ctx")
    pipe_n = lax.axis_size("pipe")
    tp_n = lax.axis_size("tp")
    assert tp_n == 4
    up, xin, q, k, v, ao = up[0].T, xin[0].T, q[0], k[0], v[0], ao[0]
    wq, wk, wv, wo = wq[0], wk[0], wv[0], wo[0]
    width, rows = up.shape
    reach = min((WINDOW - 2 + rows) // rows, ctx_n - 1)
    kv_cols, q_cols = k.shape[1], q.shape[1]
    kv_heads = kv_cols // HEAD_SIZE
    stacked = rows * (q_cols // kv_cols)
    chunks = len(chunk_cuts(width))
    groups = len(chunk_groups(chunks))
    parts = len(gather_cuts(width))
    vm = pltpu.VMEM
    dma = pltpu.SemaphoreType.DMA
    blocks = reach + 1
    own = min(reach, 1) + 1
    far = max(len(far_reach(reach)), 1)
    stats = -(-3 * kv_heads // 8) * 8
    scratch = [
        vm((tp_n, width, rows), BF),
        vm((width, rows), BF),
        vm(inv.shape, F32),
        vm(gain.shape, F32),
        vm(q.shape, BF),
        vm((blocks * rows, kv_cols), BF),
        vm((blocks * rows, kv_cols), BF),
        vm(ao.shape, BF),
        vm(wq.shape, BF),
        vm((wk.shape[0], 2 * kv_cols), BF),
        vm(wo.shape, BF),
        pltpu.SMEM(lens.shape, jnp.int32),
        vm((tp_n, wo.shape[0], width), BF),
        vm((width, rows), F32),
        vm((q_cols, rows), F32),
        vm((kv_heads, HEAD_SIZE, stacked), BF),
        vm((kv_heads, HEAD_SIZE, blocks * rows), BF),
        vm((kv_heads, HEAD_SIZE, stacked), BF),
        vm((stats, stacked), F32),
        vm((kv_heads, blocks * rows, stacked), F32),
        vm((kv_heads, blocks * rows, stacked), F32),
        vm((kv_heads, blocks * rows, stacked), BF),
        vm((far, kv_heads, HEAD_SIZE, stacked), BF),
        vm((far, kv_heads, HEAD_SIZE, stacked), BF),
        vm((far, stats, stacked), F32),
        vm((far, kv_heads, 2 * rows, stacked), F32),
        vm((kv_heads, HEAD_SIZE, own * rows), F32),
        vm((kv_heads, HEAD_SIZE, own * rows), F32),
        vm((q_cols, rows), BF),
        vm((2 * kv_cols, rows), BF),
        vm((kv_heads, HEAD_SIZE, rows), F32),
        vm((kv_heads, 2 * HEAD_SIZE, rows), BF),
        vm((kv_heads, 2 * HEAD_SIZE, rows), BF),
        vm((tp_n, width, rows), F32),
    ]
    scratch += [vm((COUPLING_ROWS + width, rows), BF)] * 6
    scratch += [vm((width, rows), BF)]
    scratch += [dma((13,))]
    scratch += [dma((max(reach, 1),))] * 3
    scratch += [dma(())]
    scratch += [dma((2 * parts + 1,))]
    scratch += [dma((far,))] * 2
    scratch += [dma((far,))]
    scratch += [dma((far, kv_heads))]
    scratch += [dma((far,))] * 2
    scratch += [dma(())]
    scratch += [dma((kv_heads,))]
    scratch += [pltpu.SemaphoreType.REGULAR] * 2
    scratch += [dma((3,))]
    scratch += [dma((1 + groups + chunks,))]
    scratch += [dma(())] * 2
    out = pl.pallas_call(
        functools.partial(kernel, ctx_n, pipe_n, reach),
        out_shape=vm((width, rows), BF),
        in_specs=[pl.BlockSpec(memory_space=pl.ANY)] * 13,
        out_specs=pl.BlockSpec(memory_space=vm),
        scratch_shapes=scratch,
        compiler_params=pltpu.CompilerParams(collective_id=0, has_side_effects=True),
        name="layer_backward",
    )(up, xin, inv, gain, q, k, v, ao, wq, wk, wv, wo, lens)
    return out.T[None]


def solution(mesh):
    placed = (
        P("pipe", "ctx", "tp"),
        P("pipe", "ctx", "tp"),
        P("pipe", "ctx"),
        P("pipe", "tp"),
        P("pipe", "ctx", "tp"),
        P("pipe", "ctx", "tp"),
        P("pipe", "ctx", "tp"),
        P("pipe", "ctx", "tp"),
        P("pipe", None, "tp"),
        P("pipe", None, "tp"),
        P("pipe", None, "tp"),
        P("pipe", "tp", None),
        P("pipe"),
    )
    return jax.shard_map(
        per_device, mesh=mesh, in_specs=placed, out_specs=P("pipe", "ctx", "tp"), check_vma=False
    )
```

```python
import functools

import jax
import jax.numpy as jnp
from jax import lax
from jax.experimental import pallas as pl
from jax.experimental.pallas import tpu as pltpu
from jax.sharding import PartitionSpec as P

QUERY_HEADS = 16
KEY_VALUE_HEADS = 8
HEAD_SIZE = 128
WINDOW = 1024
QUERY_SCALAR = 168
NEG_FILL = -1e30
GATHER_ROWS = 256
CHUNK_ROWS = 64
COUPLING_ROWS = 16
NT = (((1,), (1,)), ((), ()))
NN = (((1,), (0,)), ((), ()))
TN = (((0,), (0,)), ((), ()))
BF = jnp.bfloat16
F32 = jnp.float32


def chunk_cuts(width):
    return [(at, min(CHUNK_ROWS, width - at)) for at in range(0, width, CHUNK_ROWS)]


def gather_cuts(width):
    return [(at, min(GATHER_ROWS, width - at)) for at in range(0, width, GATHER_ROWS)]


def chunk_groups(chunks):
    edges = sorted({1, min(4, chunks), chunks})
    return [(a, b - a) for a, b in zip(edges, edges[1:])]


def direct_reach(reach):
    return [d for d in range(1, reach + 1) if d != 2]


def far_reach(reach):
    return [d for d in direct_reach(reach) if reach >= 2]


def dot(a, b, dims):
    return lax.dot_general(a, b, dims, preferred_element_type=F32)


def kernel(
    ctx_n,
    pipe_n,
    reach,
    up_h,
    xin_h,
    inv_h,
    gain_h,
    q_h,
    k_h,
    v_h,
    ao_h,
    wq_h,
    wk_h,
    wv_h,
    wo_h,
    len_h,
    out_h,
    gath,
    xin,
    inv,
    gain,
    q,
    kb,
    vb,
    ao,
    wq,
    wkv,
    wo,
    slen,
    wo_cut,
    gain_col,
    ao_t,
    q_t,
    k_t,
    do_t,
    stat,
    s,
    dp,
    ds,
    q_far,
    do_far,
    stat_far,
    s_far,
    part_v,
    part_k,
    dq_low,
    dkv,
    v_t,
    snd,
    rcv,
    pacc,
    rs_a,
    rs_ar,
    rs_b,
    rs_br,
    rs_c,
    rs_cr,
    rs_d,
    rs_dr,
    res,
    lsem,
    kv_s,
    k_r,
    v_r,
    ag_s,
    ag_r,
    q_s,
    q_r,
    do_s,
    do_r,
    st_s,
    st_r,
    acc_r,
    from_low,
    from_high,
    rs_rv,
    x_r,
):
    i = lax.axis_index("ctx")
    p = lax.axis_index("pipe")
    t = lax.axis_index("tp")
    partner = t + 1 - 2 * (t % 2)
    cross = (t + 2) % 4
    diag = 3 - t
    rows = q.shape[0]
    width = xin.shape[0]
    kv_cols = kb.shape[1]
    kv_heads = kv_cols // HEAD_SIZE
    group = q.shape[1] // kb.shape[1]
    stacked = group * rows
    scale = QUERY_SCALAR ** (-0.5)
    model_width = width * 4
    chunk = chunk_cuts(width)
    chunks = len(chunk)
    cuts = gather_cuts(width)
    direct = direct_reach(reach)
    far = far_reach(reach)

    def local(src, dst, n):
        c = pltpu.make_async_copy(src, dst, lsem.at[n])
        c.start()
        return c

    def remote(src, dst, ss, rs, dev):
        return pltpu.make_async_remote_copy(
            src_ref=src,
            dst_ref=dst,
            send_sem=ss,
            recv_sem=rs,
            device_id=dev,
            device_id_type=pl.DeviceIdType.MESH,
        )

    barrier = pltpu.get_barrier_semaphore()

    def greet(dev):
        pl.semaphore_signal(
            barrier, inc=1, device_id=dev, device_id_type=pl.DeviceIdType.MESH
        )

    has_up = i + 1 < ctx_n
    has_down = i > 0

    greet({"tp": cross})
    greet({"tp": partner})
    expect = 2
    if reach >= 1:

        @pl.when(has_down)
        def _():
            greet({"ctx": i - 1})

        @pl.when(has_up)
        def _():
            greet({"ctx": i + 1})

        expect = expect + jnp.where(has_up, 1, 0) + jnp.where(has_down, 1, 0)
    prev = (p + pipe_n - 1) % pipe_n
    if pipe_n > 1:
        greet({"pipe": prev})
        expect += 1
    if pipe_n > 2:
        greet({"pipe": (p + 1) % pipe_n})
        expect += 1

    c_q = local(q_h, q, 1)
    c_k = local(k_h, kb.at[pl.ds(0, rows)], 0)
    c_len = local(len_h, slen, 2)
    c_up = local(up_h, gath.at[t], 3)
    c_wo = local(wo_h, wo, 5)
    c_ao = local(ao_h, ao, 6)
    c_gain = local(gain_h, gain, 12)
    c_v = local(v_h, vb.at[pl.ds(0, rows)], 4)
    c_wq = local(wq_h, wq, 7)
    c_wk = local(wk_h, wkv.at[:, pl.ds(0, kv_cols)], 8)
    c_wv = local(wv_h, wkv.at[:, pl.ds(kv_cols, kv_cols)], 9)
    c_xin = local(xin_h, xin, 10)
    c_inv = local(inv_h, inv, 11)

    def head_cols(h):
        return slice(h * HEAD_SIZE, (h + 1) * HEAD_SIZE)

    def block_rows(d):
        return slice(d * rows, (d + 1) * rows)

    def flip(x):
        return x.astype(F32).T

    pl.semaphore_wait(barrier, expect)

    def kv_copy(src_h, buf, ss, rs, d):
        dst = buf.at[pl.ds(d * rows, rows)]
        if d == 2:
            return remote(buf.at[pl.ds(rows, rows)], dst, ss.at[d - 1], rs.at[d - 1], {"ctx": i + 1})
        return remote(src_h, dst, ss.at[d - 1], rs.at[d - 1], {"ctx": i + d})

    def k_copy(d):
        return kv_copy(k_h, kb, kv_s, k_r, d)

    def v_copy(d):
        return kv_copy(v_h, vb, kv_s, v_r, d)

    def sends_up(d):
        return has_up & has_down if d == 2 else i + d < ctx_n

    def q_copy(n):
        return remote(q_t, q_far.at[n], q_s.at[n], q_r.at[n], {"ctx": i - far[n]})

    def do_copy(n, g):
        return remote(
            do_t.at[g], do_far.at[n, g], do_s.at[n], do_r.at[n, g], {"ctx": i - far[n]}
        )

    def stat_copy(n):
        return remote(stat, stat_far.at[n], st_s.at[n], st_r.at[n], {"ctx": i - far[n]})

    def sends_far(n):
        return i >= 2 if far[n] == 1 else i >= far[n]

    def takes_far(n):
        return has_up & has_down if far[n] == 1 else i + far[n] < ctx_n

    if reach >= 2:
        sends_acc = has_down & has_up
        takes_acc = i + 2 < ctx_n
    else:
        sends_acc = has_down
        takes_acc = has_up

    def acc_copy(g):
        return remote(snd.at[g], rcv.at[g], lsem.at[5], acc_r.at[g], {"ctx": i - 1})

    parts = len(cuts)

    def ag_cross(n):
        sl = pl.ds(*cuts[n])
        return remote(up_h.at[sl], gath.at[t, sl], ag_s, ag_r.at[n], {"tp": cross})

    def ag_fwd(n):
        sl = pl.ds(*cuts[n])
        m = parts + n
        return remote(
            gath.at[cross, sl], gath.at[cross, sl], ag_s, ag_r.at[m], {"tp": partner}
        )

    last = pl.ds(*cuts[-1])
    ag_twin = remote(
        up_h.at[last], gath.at[t, last], ag_s, ag_r.at[2 * parts - 1], {"tp": diag}
    )
    ag_part = remote(
        up_h, gath.at[t], ag_s, ag_r.at[2 * parts], {"tp": partner}
    )
    def token(sem, cond, dev):
        @pl.when(cond)
        def _():
            pl.semaphore_signal(
                sem, inc=1, device_id=dev, device_id_type=pl.DeviceIdType.MESH
            )

    def relay(step):
        if step > 0:

            @pl.when(i >= step + 1)
            def _():
                pl.semaphore_wait(from_low, 1)

            @pl.when(i + step + 1 < ctx_n)
            def _():
                pl.semaphore_wait(from_high, 1)

        if step + 1 < reach:
            token(from_low, has_up & (i >= step + 1), {"ctx": i + 1})
            token(from_high, has_down & (i + step + 1 < ctx_n), {"ctx": i - 1})

    if reach >= 3:
        relay(0)
    for n in range(parts):
        ag_cross(n).start()
    first_core = t % 2 == 0
    if reach >= 1:

        @pl.when(has_up)
        def _():
            k_copy(1).start()
            v_copy(1).start()

    ag_part.start()
    c_q.wait()
    for g in range(kv_heads):
        for r in range(group):
            q_t[g, :, block_rows(r)] = flip(q[:, head_cols(g * group + r)]).astype(BF)

    if far:

        @pl.when(sends_far(0))
        def _():
            q_copy(0).start()


    for d in range(1, reach + 1):

        @pl.when(i < d)
        def _():
            kb[block_rows(d)] = jnp.zeros((rows, kb.shape[1]), BF)
            vb[block_rows(d)] = jnp.zeros((rows, vb.shape[1]), BF)

    c_len.wait()
    length = slen[0]
    key_i = lax.broadcasted_iota(jnp.int32, (rows, stacked), 0)
    qry_i = lax.broadcasted_iota(jnp.int32, (rows, stacked), 1) % rows
    later0 = qry_i - key_i
    pos_q = i * rows + qry_i
    live = (pos_q < length)[:1]

    def allowed(query_pos, d):
        later = later0 + d * rows
        pos_k = query_pos - later
        ok = (later >= 0) & (later < WINDOW) & (pos_k < length) & (query_pos < length)
        return ok & (pos_k >= 0)

    def scores(d):
        ok = allowed(pos_q, d)
        for g in range(kv_heads):
            keys = kb[block_rows(d), head_cols(g)]
            sc = dot(keys, q_t[g], NN) * scale
            s[g, block_rows(d)] = jnp.where(ok, sc, NEG_FILL)
            k_t[g, :, block_rows(d)] = flip(keys).astype(BF)

    c_k.wait()
    scores(0)
    c_wo.wait()
    for n in range(4):
        wo_cut[n] = wo[:, n * width : (n + 1) * width]
    c_ao.wait()
    for h in range(kv_heads * group):
        ao_t[head_cols(h), :] = flip(ao[:, head_cols(h)])
    c_v.wait()
    for g in range(kv_heads):
        v_t[g] = flip(vb[:rows, head_cols(g)])
    c_gain.wait()
    gain_col[...] = jnp.broadcast_to(gain[...], (rows, width)).T
    if reach >= 3:
        relay(1)

    def shard_dot(owner, n):
        at, size = cuts[n]
        return dot(wo_cut[owner, :, at : at + size], gath[owner, at : at + size], NN)

    c_up.wait()
    acc = dot(wo_cut[t], gath[t], NN)
    ag_part.wait_recv()

    @pl.when(first_core)
    def _():
        ag_twin.start()

    acc = acc + dot(wo_cut[partner], gath[partner], NN)

    for step in range(2, reach):
        relay(step)
    for d in direct[1:]:

        @pl.when(sends_up(d))
        def _():
            k_copy(d).start()

    for n in range(1, len(far)):

        @pl.when(sends_far(n))
        def _():
            q_copy(n).start()

    def take(copy, d):
        @pl.when(i >= d)
        def _():
            copy(d).wait_recv()

    def pass_on(copy):
        if reach >= 2:

            @pl.when(sends_up(2))
            def _():
                copy(2).start()

    if reach >= 1:
        take(k_copy, 1)
        pass_on(k_copy)
        scores(1)

    for n in range(parts):
        ag_cross(n).wait_recv()
        if n + 1 < parts:
            ag_fwd(n).start()
        else:
            pl.when(jnp.logical_not(first_core))(ag_fwd(n).start)
        acc = acc + shard_dot(cross, n)
    for n in range(parts):
        if n + 1 == parts and reach >= 1:
            take(v_copy, 1)
            pass_on(v_copy)
        ag_fwd(n).wait_recv()
        acc = acc + shard_dot(diag, n)
    grad = acc.astype(BF)
    for g in range(kv_heads):
        for r in range(group):
            do_t[g, :, block_rows(r)] = grad[head_cols(g * group + r)]

    def send_dout(n, heads):
        @pl.when(sends_far(n))
        def _():
            for g in heads:
                do_copy(n, g).start()

    def send_stat(n):
        @pl.when(sends_far(n))
        def _():
            stat_copy(n).start()

    if far:
        send_dout(0, range(1))

    for g in range(kv_heads):
        sums = []
        for r in range(group):
            h = g * group + r
            sums.append(
                jnp.sum(
                    grad[head_cols(h)].astype(F32) * ao_t[head_cols(h), :], axis=0, keepdims=True
                )
            )
        stat[3 * g + 2 : 3 * g + 3, :] = jnp.concatenate(sums, axis=1)

    for d in range(2, reach + 1):
        take(k_copy, d)
        scores(d)

    for g in range(kv_heads):
        top = jnp.max(s[g], axis=0, keepdims=True)
        total = jnp.zeros((1, stacked), F32)
        for d in range(reach + 1):
            e = jnp.exp(s[g, block_rows(d)] - top)
            s[g, block_rows(d)] = e
            total = total + jnp.sum(e, axis=0, keepdims=True)
        inv_total = jnp.where(live, 1.0 / total, 0.0)
        for d in range(reach + 1):
            s[g, block_rows(d)] = s[g, block_rows(d)] * inv_total
        stat[3 * g : 3 * g + 1, :] = top
        stat[3 * g + 1 : 3 * g + 2, :] = inv_total

    if far:
        send_stat(0)
        for n in range(1, len(far)):
            send_dout(n, range(1))
            send_stat(n)
        for n in range(len(far)):
            send_dout(n, range(1, kv_heads))
    for d in direct[1:]:

        @pl.when(sends_up(d))
        def _():
            v_copy(d).start()

    for d in range(2, reach + 1):
        take(v_copy, d)

    own = min(reach, 1) + 1
    for g in range(kv_heads):
        dp[g] = dot(vb[:, head_cols(g)], do_t[g], NN)
        part_v[g] = dot(do_t[g], s[g, : own * rows].astype(BF), NT)
        delta = stat[3 * g + 2 : 3 * g + 3, :]
        for d in range(reach + 1):
            ds[g, block_rows(d)] = (
                s[g, block_rows(d)] * (dp[g, block_rows(d)] - delta)
            ).astype(BF)
        part_k[g] = dot(q_t[g], ds[g, : own * rows], NT)

    def send_acc(g):
        snd[g, :HEAD_SIZE] = part_v[g, :, block_rows(1)].astype(BF)
        snd[g, HEAD_SIZE:] = part_k[g, :, block_rows(1)].astype(BF)
        acc_copy(g).start()

    if reach == 1:

        @pl.when(has_down)
        def _():
            for g in range(kv_heads):
                send_acc(g)

    if reach >= 2:

        @pl.when(i != 1)
        def _():
            part_v[:, :, block_rows(1)] = jnp.zeros((kv_heads, HEAD_SIZE, rows), F32)
            part_k[:, :, block_rows(1)] = jnp.zeros((kv_heads, HEAD_SIZE, rows), F32)

    coupling = jnp.zeros((1, rows), F32)
    low = []
    for g in range(kv_heads):
        dq = dot(k_t[g], ds[g], NN) * scale
        for r in range(group):
            part = dq[:, block_rows(r)].astype(BF)
            low.append(part)
            coupling = coupling + jnp.sum(
                part.astype(F32) * q_t[g, :, block_rows(r)].astype(F32), axis=0, keepdims=True
            )
    dq_low[...] = jnp.concatenate(low, axis=0)
    owners = (diag, cross, partner, t)

    def piece_rows(n, at=0, size=width):
        return pl.ds(pl.multiple_of(owners[n] * width + at, 16), size)

    def far_blocks(n):
        return ((1, 2), (0, 1)) if far[n] == 1 else ((0, far[n]),)

    def far_scores(n):
        @pl.when(takes_far(n))
        def _():
            q_copy(n).wait_recv()
            for at, (kd, dist) in enumerate(far_blocks(n)):
                ok = allowed((i + far[n]) * rows + qry_i, dist)
                for g in range(kv_heads):
                    sc = dot(kb[block_rows(kd), head_cols(g)], q_far[n, g], NN) * scale
                    s_far[n, g, block_rows(at)] = jnp.where(ok, sc, NEG_FILL)

    def far_pair(n):
        @pl.when(takes_far(n))
        def _():
            stat_copy(n).wait_recv()
            for at in range(len(far_blocks(n))):
                for g in range(kv_heads):
                    top = stat_far[n, 3 * g : 3 * g + 1, :]
                    inv_total = stat_far[n, 3 * g + 1 : 3 * g + 2, :]
                    s_far[n, g, block_rows(at)] = (
                        jnp.exp(s_far[n, g, block_rows(at)] - top) * inv_total
                    )
            for g in range(kv_heads):
                delta = stat_far[n, 3 * g + 2 : 3 * g + 3, :]
                do_copy(n, g).wait_recv()
                for at, (kd, _) in enumerate(far_blocks(n)):
                    pr = s_far[n, g, block_rows(at)]
                    part_v[g, :, block_rows(kd)] += dot(do_far[n, g], pr.astype(BF), NT)
                    dprob = dot(vb[block_rows(kd), head_cols(g)], do_far[n, g], NN)
                    dsc = (pr * (dprob - delta)).astype(BF)
                    part_k[g, :, block_rows(kd)] += dot(q_far[n, g], dsc, NT)
                    if kd == 1:
                        send_acc(g)

    def project_query():
        c_wq.wait()
        for n in range(4):
            pacc[n] = dot(wq[piece_rows(n), :], dq_low[...], NN)

    if far:
        early = i < 2
        far_scores(0)
        pl.when(early)(project_query)
        far_pair(0)
        pl.when(jnp.logical_not(early))(project_query)
    else:
        project_query()
    for n in range(1, len(far)):
        far_scores(n)
    for n in range(1, len(far)):
        far_pair(n)
    c_wk.wait()
    c_wv.wait()
    c_xin.wait()
    c_inv.wait()
    if reach >= 1:

        @pl.when(takes_acc)
        def _():
            for g in range(kv_heads):
                acc_copy(g).wait_recv()
                part_v[g, :, :rows] += rcv[g, :HEAD_SIZE].astype(F32)
                part_k[g, :, :rows] += rcv[g, HEAD_SIZE:].astype(F32)

    for g in range(kv_heads):
        dk_low = (part_k[g, :, :rows] * scale).astype(BF)
        dv_low = part_v[g, :, :rows].astype(BF)
        dkv[head_cols(g), :] = dk_low
        dkv[head_cols(kv_heads + g), :] = dv_low
        both = dk_low.astype(F32) * k_t[g, :, :rows].astype(F32) + dv_low.astype(F32) * v_t[g]
        coupling = coupling + jnp.sum(both, axis=0, keepdims=True)

    def piece(n, at=0, size=width):
        return pacc[n, at : at + size] + dot(wkv[piece_rows(n, at, size), :], dkv[...], NN)

    lead = COUPLING_ROWS
    wide = jnp.broadcast_to(coupling, (lead, rows))

    def span_of(first, count=1):
        at, size = chunk[first][0], sum(chunk[n][1] for n in range(first, first + count))
        return (0, lead + size) if first == 0 else (lead + at, size)

    groups = chunk_groups(chunks)

    def a_copy(m):
        sl = pl.ds(*span_of(*groups[m]))
        return remote(rs_a.at[sl], rs_ar.at[sl], lsem.at[0], rs_rv.at[1 + m], {"tp": partner})

    send_c = remote(rs_c, rs_cr, lsem.at[1], rs_rv.at[0], {"tp": partner})
    base = 1 + len(groups)
    head = chunk[0][1]
    send_d = remote(rs_d, rs_dr, lsem.at[6], rs_rv.at[base + chunks], {"tp": diag})

    def b_copy(n):
        sl = pl.ds(*span_of(n))
        return remote(rs_b.at[sl], rs_br.at[sl], lsem.at[3], rs_rv.at[base + n], {"tp": cross})

    def x_copy(at, size):
        sl = pl.ds(at, size)
        if pipe_n == 1:
            return pltpu.make_async_copy(res.at[sl], out_h.at[sl], lsem.at[12])
        return remote(res.at[sl], out_h.at[sl], lsem.at[12], x_r, {"pipe": prev})

    def send_a(m):
        first, count = groups[m]
        at, size = chunk[first][0], sum(chunk[n][1] for n in range(first, first + count))
        rs_a[lead + at : lead + at + size, :] = piece(0, at, size).astype(BF)
        a_copy(m).start()

    send_a(0)
    rs_d[:lead, :] = wide.astype(BF)
    rs_d[lead:, :] = piece(0, 0, head).astype(BF)
    send_d.start()
    rs_b[:lead, :] = wide.astype(BF)
    rs_b[lead : lead + head, :] = piece(1, 0, head).astype(BF)
    b_copy(0).start()
    for m in range(1, len(groups)):
        send_a(m)
    for m, (first, count) in enumerate(groups):
        at, size = chunk[first][0], sum(chunk[n][1] for n in range(first, first + count))
        pacc[1, at : at + size] = piece(1, at, size)
        a_copy(m).wait_recv()
        for n in range(first, first + count):
            at, size = chunk[n]
            sl = slice(at, at + size)
            sh = slice(lead + at, lead + at + size)
            rs_b[sh, :] = (pacc[1, sl] + rs_ar[sh, :].astype(F32)).astype(BF)
            b_copy(n).start()
        if m == 0:
            rs_c[lead:, :] = piece(2).astype(BF)
            rs_c[:lead, :] = wide.astype(BF)
            send_c.start()
    pacc[3] = piece(3)
    iv = inv[...]
    send_c.wait_recv()
    for n in range(chunks):
        at, size = chunk[n]
        sl = slice(at, at + size)
        sh = slice(lead + at, lead + at + size)
        b_copy(n).wait_recv()
        normed = pacc[3, sl] + rs_cr[sh, :].astype(F32) + rs_br[sh, :].astype(F32)
        if n == 0:
            send_d.wait_recv()
            coup = coupling + rs_cr[:lead, :].astype(F32)[:1]
            coup = coup + rs_br[:lead, :].astype(F32)[:1] + rs_dr[:lead, :].astype(F32)[:1]
            drag = iv * coup / model_width
            normed = normed + rs_dr[lead:, :].astype(F32)
        val = gath[t, sl, :].astype(F32) + iv * (
            gain_col[sl, :] * normed - xin[sl, :].astype(F32) * drag
        )
        res[sl, :] = val.astype(BF)
        x_copy(at, size).start()

    shards = gath.at[pl.ds(0, 3)]
    remote(shards, shards, ag_s, ag_r.at[0], {"tp": partner}).wait_send()
    for d in range(1, reach + 1):

        @pl.when(sends_up(d))
        def _():
            both_blocks = kb.at[pl.ds(0, 2 * rows)]
            remote(
                both_blocks, both_blocks, kv_s.at[d - 1], k_r.at[d - 1], {"ctx": i + 1}
            ).wait_send()

    for n in range(len(far)):

        @pl.when(sends_far(n))
        def _():
            q_copy(n).wait_send()
            stat_copy(n).wait_send()
            remote(
                do_t, do_far.at[n], do_s.at[n], do_r.at[n, 0], {"ctx": i - far[n]}
            ).wait_send()

    if reach >= 1:

        @pl.when(sends_acc)
        def _():
            remote(snd, rcv, lsem.at[5], acc_r.at[0], {"ctx": i - 1}).wait_send()

    send_c.wait_send()
    send_d.wait_send()
    rest = pl.ds(lead + head, width - head)
    remote(
        rs_a.at[rest], rs_ar.at[rest], lsem.at[0], rs_rv.at[1], {"tp": partner}
    ).wait_send()
    remote(rs_b, rs_br, lsem.at[3], rs_rv.at[base], {"tp": cross}).wait_send()
    x_copy(0, width).wait()


def per_device(up, xin, inv, gain, q, k, v, ao, wq, wk, wv, wo, lens):
    ctx_n = lax.axis_size("ctx")
    pipe_n = lax.axis_size("pipe")
    tp_n = lax.axis_size("tp")
    assert tp_n == 4
    up, xin, q, k, v, ao = up[0].T, xin[0].T, q[0], k[0], v[0], ao[0]
    wq, wk, wv, wo = wq[0], wk[0], wv[0], wo[0]
    width, rows = up.shape
    reach = min((WINDOW - 2 + rows) // rows, ctx_n - 1)
    kv_cols, q_cols = k.shape[1], q.shape[1]
    kv_heads = kv_cols // HEAD_SIZE
    stacked = rows * (q_cols // kv_cols)
    chunks = len(chunk_cuts(width))
    groups = len(chunk_groups(chunks))
    parts = len(gather_cuts(width))
    vm = pltpu.VMEM
    dma = pltpu.SemaphoreType.DMA
    blocks = reach + 1
    own = min(reach, 1) + 1
    far = max(len(far_reach(reach)), 1)
    stats = -(-3 * kv_heads // 8) * 8
    scratch = [
        vm((tp_n, width, rows), BF),
        vm((width, rows), BF),
        vm(inv.shape, F32),
        vm(gain.shape, F32),
        vm(q.shape, BF),
        vm((blocks * rows, kv_cols), BF),
        vm((blocks * rows, kv_cols), BF),
        vm(ao.shape, BF),
        vm(wq.shape, BF),
        vm((wk.shape[0], 2 * kv_cols), BF),
        vm(wo.shape, BF),
        pltpu.SMEM(lens.shape, jnp.int32),
        vm((tp_n, wo.shape[0], width), BF),
        vm((width, rows), F32),
        vm((q_cols, rows), F32),
        vm((kv_heads, HEAD_SIZE, stacked), BF),
        vm((kv_heads, HEAD_SIZE, blocks * rows), BF),
        vm((kv_heads, HEAD_SIZE, stacked), BF),
        vm((stats, stacked), F32),
        vm((kv_heads, blocks * rows, stacked), F32),
        vm((kv_heads, blocks * rows, stacked), F32),
        vm((kv_heads, blocks * rows, stacked), BF),
        vm((far, kv_heads, HEAD_SIZE, stacked), BF),
        vm((far, kv_heads, HEAD_SIZE, stacked), BF),
        vm((far, stats, stacked), F32),
        vm((far, kv_heads, 2 * rows, stacked), F32),
        vm((kv_heads, HEAD_SIZE, own * rows), F32),
        vm((kv_heads, HEAD_SIZE, own * rows), F32),
        vm((q_cols, rows), BF),
        vm((2 * kv_cols, rows), BF),
        vm((kv_heads, HEAD_SIZE, rows), F32),
        vm((kv_heads, 2 * HEAD_SIZE, rows), BF),
        vm((kv_heads, 2 * HEAD_SIZE, rows), BF),
        vm((tp_n, width, rows), F32),
    ]
    scratch += [vm((COUPLING_ROWS + width, rows), BF)] * 6
    scratch += [vm((COUPLING_ROWS + chunk_cuts(width)[0][1], rows), BF)] * 2
    scratch += [vm((width, rows), BF)]
    scratch += [dma((13,))]
    scratch += [dma((max(reach, 1),))] * 3
    scratch += [dma(())]
    scratch += [dma((2 * parts + 1,))]
    scratch += [dma((far,))] * 2
    scratch += [dma((far,))]
    scratch += [dma((far, kv_heads))]
    scratch += [dma((far,))] * 2
    scratch += [dma((kv_heads,))]
    scratch += [pltpu.SemaphoreType.REGULAR] * 2
    scratch += [dma((2 + groups + chunks,))]
    scratch += [dma(())]
    out = pl.pallas_call(
        functools.partial(kernel, ctx_n, pipe_n, reach),
        out_shape=vm((width, rows), BF),
        in_specs=[pl.BlockSpec(memory_space=pl.ANY)] * 13,
        out_specs=pl.BlockSpec(memory_space=vm),
        scratch_shapes=scratch,
        compiler_params=pltpu.CompilerParams(collective_id=0, has_side_effects=True),
        name="layer_backward",
    )(up, xin, inv, gain, q, k, v, ao, wq, wk, wv, wo, lens)
    return out.T[None]


def solution(mesh):
    placed = (
        P("pipe", "ctx", "tp"),
        P("pipe", "ctx", "tp"),
        P("pipe", "ctx"),
        P("pipe", "tp"),
        P("pipe", "ctx", "tp"),
        P("pipe", "ctx", "tp"),
        P("pipe", "ctx", "tp"),
        P("pipe", "ctx", "tp"),
        P("pipe", None, "tp"),
        P("pipe", None, "tp"),
        P("pipe", None, "tp"),
        P("pipe", "tp", None),
        P("pipe"),
    )
    return jax.shard_map(
        per_device, mesh=mesh, in_specs=placed, out_specs=P("pipe", "ctx", "tp"), check_vma=False
    )
```

```python
import functools

import jax
import jax.numpy as jnp
from jax import lax
from jax.experimental import pallas as pl
from jax.experimental.pallas import tpu as pltpu
from jax.sharding import PartitionSpec as P

QUERY_HEADS = 16
KEY_VALUE_HEADS = 8
HEAD_SIZE = 128
WINDOW = 1024
QUERY_SCALAR = 168
NEG_FILL = -1e30
GATHER_ROWS = 256
CHUNK_ROWS = 64
COUPLING_ROWS = 16
NT = (((1,), (1,)), ((), ()))
NN = (((1,), (0,)), ((), ()))
TN = (((0,), (0,)), ((), ()))
BF = jnp.bfloat16
F32 = jnp.float32


def chunk_cuts(width):
    return [(at, min(CHUNK_ROWS, width - at)) for at in range(0, width, CHUNK_ROWS)]


def gather_cuts(width):
    return [(at, min(GATHER_ROWS, width - at)) for at in range(0, width, GATHER_ROWS)]


def chunk_groups(chunks):
    edges = sorted({1, min(4, chunks), chunks})
    return [(a, b - a) for a, b in zip(edges, edges[1:])]


def direct_reach(reach):
    return [d for d in range(1, reach + 1) if d != 2]


def far_reach(reach):
    return [d for d in direct_reach(reach) if reach >= 2]


def dot(a, b, dims):
    return lax.dot_general(a, b, dims, preferred_element_type=F32)


def kernel(
    ctx_n,
    pipe_n,
    reach,
    up_h,
    xin_h,
    inv_h,
    gain_h,
    q_h,
    k_h,
    v_h,
    ao_h,
    wq_h,
    wk_h,
    wv_h,
    wo_h,
    len_h,
    out_h,
    gath,
    xin,
    inv,
    gain,
    q,
    kb,
    vb,
    ao,
    wq,
    wkv,
    wo,
    slen,
    wo_cut,
    gain_col,
    ao_t,
    q_t,
    k_t,
    do_t,
    stat,
    s,
    dp,
    ds,
    q_far,
    do_far,
    stat_far,
    s_far,
    part_v,
    part_k,
    dq_low,
    dkv,
    v_t,
    snd,
    rcv,
    pacc,
    rs_a,
    rs_ar,
    rs_b,
    rs_br,
    rs_c,
    rs_cr,
    rs_d,
    rs_dr,
    res,
    lsem,
    kv_s,
    k_r,
    v_r,
    ag_s,
    ag_r,
    q_s,
    q_r,
    do_s,
    do_r,
    st_s,
    st_r,
    acc_r,
    from_low,
    from_high,
    rs_rv,
    x_r,
):
    i = lax.axis_index("ctx")
    p = lax.axis_index("pipe")
    t = lax.axis_index("tp")
    partner = t + 1 - 2 * (t % 2)
    cross = (t + 2) % 4
    diag = 3 - t
    rows = q.shape[0]
    width = xin.shape[0]
    kv_cols = kb.shape[1]
    kv_heads = kv_cols // HEAD_SIZE
    group = q.shape[1] // kb.shape[1]
    stacked = group * rows
    scale = QUERY_SCALAR ** (-0.5)
    model_width = width * 4
    chunk = chunk_cuts(width)
    chunks = len(chunk)
    cuts = gather_cuts(width)
    direct = direct_reach(reach)
    far = far_reach(reach)

    def local(src, dst, n):
        c = pltpu.make_async_copy(src, dst, lsem.at[n])
        c.start()
        return c

    def remote(src, dst, ss, rs, dev):
        return pltpu.make_async_remote_copy(
            src_ref=src,
            dst_ref=dst,
            send_sem=ss,
            recv_sem=rs,
            device_id=dev,
            device_id_type=pl.DeviceIdType.MESH,
        )

    barrier = pltpu.get_barrier_semaphore()

    def greet(dev):
        pl.semaphore_signal(
            barrier, inc=1, device_id=dev, device_id_type=pl.DeviceIdType.MESH
        )

    has_up = i + 1 < ctx_n
    has_down = i > 0

    greet({"tp": cross})
    greet({"tp": partner})
    expect = 2
    if reach >= 1:

        @pl.when(has_down)
        def _():
            greet({"ctx": i - 1})

        @pl.when(has_up)
        def _():
            greet({"ctx": i + 1})

        expect = expect + jnp.where(has_up, 1, 0) + jnp.where(has_down, 1, 0)
    prev = (p + pipe_n - 1) % pipe_n
    if pipe_n > 1:
        greet({"pipe": prev})
        expect += 1
    if pipe_n > 2:
        greet({"pipe": (p + 1) % pipe_n})
        expect += 1

    c_q = local(q_h, q, 1)
    c_k = local(k_h, kb.at[pl.ds(0, rows)], 0)
    c_len = local(len_h, slen, 2)
    c_up = local(up_h, gath.at[t], 3)
    c_wo = local(wo_h, wo, 5)
    c_ao = local(ao_h, ao, 6)
    c_gain = local(gain_h, gain, 12)
    c_v = local(v_h, vb.at[pl.ds(0, rows)], 4)
    c_wq = local(wq_h, wq, 7)
    c_wk = local(wk_h, wkv.at[:, pl.ds(0, kv_cols)], 8)
    c_wv = local(wv_h, wkv.at[:, pl.ds(kv_cols, kv_cols)], 9)
    c_xin = local(xin_h, xin, 10)
    c_inv = local(inv_h, inv, 11)

    def head_cols(h):
        return slice(h * HEAD_SIZE, (h + 1) * HEAD_SIZE)

    def block_rows(d):
        return slice(d * rows, (d + 1) * rows)

    def flip(x):
        return x.astype(F32).T

    pl.semaphore_wait(barrier, expect)

    def kv_copy(src_h, buf, ss, rs, d):
        dst = buf.at[pl.ds(d * rows, rows)]
        if d == 2:
            return remote(buf.at[pl.ds(rows, rows)], dst, ss.at[d - 1], rs.at[d - 1], {"ctx": i + 1})
        return remote(src_h, dst, ss.at[d - 1], rs.at[d - 1], {"ctx": i + d})

    def k_copy(d):
        return kv_copy(k_h, kb, kv_s, k_r, d)

    def v_copy(d):
        return kv_copy(v_h, vb, kv_s, v_r, d)

    def sends_up(d):
        return has_up & has_down if d == 2 else i + d < ctx_n

    def q_copy(n):
        return remote(q_t, q_far.at[n], q_s.at[n], q_r.at[n], {"ctx": i - far[n]})

    def do_copy(n, g):
        return remote(
            do_t.at[g], do_far.at[n, g], do_s.at[n], do_r.at[n, g], {"ctx": i - far[n]}
        )

    def stat_copy(n):
        return remote(stat, stat_far.at[n], st_s.at[n], st_r.at[n], {"ctx": i - far[n]})

    def sends_far(n):
        return i >= 2 if far[n] == 1 else i >= far[n]

    def takes_far(n):
        return has_up & has_down if far[n] == 1 else i + far[n] < ctx_n

    if reach >= 2:
        sends_acc = has_down & has_up
        takes_acc = i + 2 < ctx_n
    else:
        sends_acc = has_down
        takes_acc = has_up

    def acc_copy(g):
        return remote(snd.at[g], rcv.at[g], lsem.at[5], acc_r.at[g], {"ctx": i - 1})

    parts = len(cuts)

    def ag_cross(n):
        sl = pl.ds(*cuts[n])
        return remote(up_h.at[sl], gath.at[t, sl], ag_s, ag_r.at[n], {"tp": cross})

    def ag_fwd(n):
        sl = pl.ds(*cuts[n])
        m = parts + n
        return remote(
            gath.at[cross, sl], gath.at[cross, sl], ag_s, ag_r.at[m], {"tp": partner}
        )

    last = pl.ds(*cuts[-1])
    ag_twin = remote(
        up_h.at[last], gath.at[t, last], ag_s, ag_r.at[2 * parts - 1], {"tp": diag}
    )
    ag_part = remote(
        up_h, gath.at[t], ag_s, ag_r.at[2 * parts], {"tp": partner}
    )
    def token(sem, cond, dev):
        @pl.when(cond)
        def _():
            pl.semaphore_signal(
                sem, inc=1, device_id=dev, device_id_type=pl.DeviceIdType.MESH
            )

    def relay(step):
        if step > 0:

            @pl.when(i >= step + 1)
            def _():
                pl.semaphore_wait(from_low, 1)

            @pl.when(i + step + 1 < ctx_n)
            def _():
                pl.semaphore_wait(from_high, 1)

        if step + 1 < reach:
            token(from_low, has_up & (i >= step + 1), {"ctx": i + 1})
            token(from_high, has_down & (i + step + 1 < ctx_n), {"ctx": i - 1})

    if reach >= 3:
        relay(0)
    for n in range(parts):
        ag_cross(n).start()
    first_core = t % 2 == 0
    if reach >= 1:

        @pl.when(has_up)
        def _():
            k_copy(1).start()
            v_copy(1).start()

    ag_part.start()
    c_q.wait()
    for g in range(kv_heads):
        for r in range(group):
            q_t[g, :, block_rows(r)] = flip(q[:, head_cols(g * group + r)]).astype(BF)

    if far:

        @pl.when(sends_far(0))
        def _():
            q_copy(0).start()


    for d in range(1, reach + 1):

        @pl.when(i < d)
        def _():
            kb[block_rows(d)] = jnp.zeros((rows, kb.shape[1]), BF)
            vb[block_rows(d)] = jnp.zeros((rows, vb.shape[1]), BF)

    c_len.wait()
    length = slen[0]
    key_i = lax.broadcasted_iota(jnp.int32, (rows, stacked), 0)
    qry_i = lax.broadcasted_iota(jnp.int32, (rows, stacked), 1) % rows
    later0 = qry_i - key_i
    pos_q = i * rows + qry_i
    live = (pos_q < length)[:1]

    def allowed(query_pos, d):
        later = later0 + d * rows
        pos_k = query_pos - later
        ok = (later >= 0) & (later < WINDOW) & (pos_k < length) & (query_pos < length)
        return ok & (pos_k >= 0)

    def scores(d):
        ok = allowed(pos_q, d)
        for g in range(kv_heads):
            keys = kb[block_rows(d), head_cols(g)]
            sc = dot(keys, q_t[g], NN) * scale
            s[g, block_rows(d)] = jnp.where(ok, sc, NEG_FILL)
            k_t[g, :, block_rows(d)] = flip(keys).astype(BF)

    c_k.wait()
    scores(0)
    c_wo.wait()
    for n in range(4):
        wo_cut[n] = wo[:, n * width : (n + 1) * width]
    c_ao.wait()
    for h in range(kv_heads * group):
        ao_t[head_cols(h), :] = flip(ao[:, head_cols(h)])
    c_v.wait()
    for g in range(kv_heads):
        v_t[g] = flip(vb[:rows, head_cols(g)])
    c_gain.wait()
    gain_col[...] = jnp.broadcast_to(gain[...], (rows, width)).T
    if reach >= 3:
        relay(1)

    def shard_dot(owner, n):
        at, size = cuts[n]
        return dot(wo_cut[owner, :, at : at + size], gath[owner, at : at + size], NN)

    c_up.wait()
    acc = dot(wo_cut[t], gath[t], NN)
    ag_part.wait_recv()

    @pl.when(first_core)
    def _():
        ag_twin.start()

    acc = acc + dot(wo_cut[partner], gath[partner], NN)

    for step in range(2, reach):
        relay(step)
    for d in direct[1:]:

        @pl.when(sends_up(d))
        def _():
            k_copy(d).start()

    for n in range(1, len(far)):

        @pl.when(sends_far(n))
        def _():
            q_copy(n).start()

    def take(copy, d):
        @pl.when(i >= d)
        def _():
            copy(d).wait_recv()

    def pass_on(copy):
        if reach >= 2:

            @pl.when(sends_up(2))
            def _():
                copy(2).start()

    if reach >= 1:
        take(k_copy, 1)
        pass_on(k_copy)
        scores(1)

    for n in range(parts):
        ag_cross(n).wait_recv()
        if n + 1 < parts:
            ag_fwd(n).start()
        else:
            pl.when(jnp.logical_not(first_core))(ag_fwd(n).start)
        acc = acc + shard_dot(cross, n)
    for n in range(parts):
        if n + 1 == parts and reach >= 1:
            take(v_copy, 1)
            pass_on(v_copy)
        ag_fwd(n).wait_recv()
        acc = acc + shard_dot(diag, n)
    grad = acc.astype(BF)
    for g in range(kv_heads):
        for r in range(group):
            do_t[g, :, block_rows(r)] = grad[head_cols(g * group + r)]

    def send_dout(n, heads):
        @pl.when(sends_far(n))
        def _():
            for g in heads:
                do_copy(n, g).start()

    def send_stat(n):
        @pl.when(sends_far(n))
        def _():
            stat_copy(n).start()

    if far:
        send_dout(0, range(1))

    for g in range(kv_heads):
        sums = []
        for r in range(group):
            h = g * group + r
            sums.append(
                jnp.sum(
                    grad[head_cols(h)].astype(F32) * ao_t[head_cols(h), :], axis=0, keepdims=True
                )
            )
        stat[3 * g + 2 : 3 * g + 3, :] = jnp.concatenate(sums, axis=1)

    for d in range(2, reach + 1):
        take(k_copy, d)
        scores(d)

    for g in range(kv_heads):
        top = jnp.max(s[g], axis=0, keepdims=True)
        total = jnp.zeros((1, stacked), F32)
        for d in range(reach + 1):
            e = jnp.exp(s[g, block_rows(d)] - top)
            s[g, block_rows(d)] = e
            total = total + jnp.sum(e, axis=0, keepdims=True)
        inv_total = jnp.where(live, 1.0 / total, 0.0)
        for d in range(reach + 1):
            s[g, block_rows(d)] = s[g, block_rows(d)] * inv_total
        stat[3 * g : 3 * g + 1, :] = top
        stat[3 * g + 1 : 3 * g + 2, :] = inv_total

    if far:
        send_stat(0)
        for n in range(1, len(far)):
            send_dout(n, range(1))
            send_stat(n)
        for n in reversed(range(len(far))):
            send_dout(n, range(1, kv_heads))
    for d in direct[1:]:

        @pl.when(sends_up(d))
        def _():
            v_copy(d).start()

    for d in range(2, reach + 1):
        take(v_copy, d)

    own = min(reach, 1) + 1
    for g in range(kv_heads):
        dp[g] = dot(vb[:, head_cols(g)], do_t[g], NN)
        part_v[g] = dot(do_t[g], s[g, : own * rows].astype(BF), NT)
        delta = stat[3 * g + 2 : 3 * g + 3, :]
        for d in range(reach + 1):
            ds[g, block_rows(d)] = (
                s[g, block_rows(d)] * (dp[g, block_rows(d)] - delta)
            ).astype(BF)
        part_k[g] = dot(q_t[g], ds[g, : own * rows], NT)

    def send_acc(g):
        snd[g, :HEAD_SIZE] = part_v[g, :, block_rows(1)].astype(BF)
        snd[g, HEAD_SIZE:] = part_k[g, :, block_rows(1)].astype(BF)
        acc_copy(g).start()

    if reach == 1:

        @pl.when(has_down)
        def _():
            for g in range(kv_heads):
                send_acc(g)

    if reach >= 2:

        @pl.when(i != 1)
        def _():
            part_v[:, :, block_rows(1)] = jnp.zeros((kv_heads, HEAD_SIZE, rows), F32)
            part_k[:, :, block_rows(1)] = jnp.zeros((kv_heads, HEAD_SIZE, rows), F32)

    coupling = jnp.zeros((1, rows), F32)
    low = []
    for g in range(kv_heads):
        dq = dot(k_t[g], ds[g], NN) * scale
        for r in range(group):
            part = dq[:, block_rows(r)].astype(BF)
            low.append(part)
            coupling = coupling + jnp.sum(
                part.astype(F32) * q_t[g, :, block_rows(r)].astype(F32), axis=0, keepdims=True
            )
    dq_low[...] = jnp.concatenate(low, axis=0)
    owners = (diag, cross, partner, t)

    def piece_rows(n, at=0, size=width):
        return pl.ds(pl.multiple_of(owners[n] * width + at, 16), size)

    def far_blocks(n):
        return ((1, 2), (0, 1)) if far[n] == 1 else ((0, far[n]),)

    def far_scores(n):
        @pl.when(takes_far(n))
        def _():
            q_copy(n).wait_recv()
            for at, (kd, dist) in enumerate(far_blocks(n)):
                ok = allowed((i + far[n]) * rows + qry_i, dist)
                for g in range(kv_heads):
                    sc = dot(kb[block_rows(kd), head_cols(g)], q_far[n, g], NN) * scale
                    s_far[n, g, block_rows(at)] = jnp.where(ok, sc, NEG_FILL)

    def far_pair(n):
        @pl.when(takes_far(n))
        def _():
            stat_copy(n).wait_recv()
            for at in range(len(far_blocks(n))):
                for g in range(kv_heads):
                    top = stat_far[n, 3 * g : 3 * g + 1, :]
                    inv_total = stat_far[n, 3 * g + 1 : 3 * g + 2, :]
                    s_far[n, g, block_rows(at)] = (
                        jnp.exp(s_far[n, g, block_rows(at)] - top) * inv_total
                    )
            for g in range(kv_heads):
                delta = stat_far[n, 3 * g + 2 : 3 * g + 3, :]
                do_copy(n, g).wait_recv()
                for at, (kd, _) in enumerate(far_blocks(n)):
                    pr = s_far[n, g, block_rows(at)]
                    part_v[g, :, block_rows(kd)] += dot(do_far[n, g], pr.astype(BF), NT)
                    dprob = dot(vb[block_rows(kd), head_cols(g)], do_far[n, g], NN)
                    dsc = (pr * (dprob - delta)).astype(BF)
                    part_k[g, :, block_rows(kd)] += dot(q_far[n, g], dsc, NT)
                    if kd == 1:
                        send_acc(g)

    def project_query():
        c_wq.wait()
        for n in range(4):
            pacc[n] = dot(wq[piece_rows(n), :], dq_low[...], NN)

    if far:
        early = i < 2
        far_scores(0)
        pl.when(early)(project_query)
        far_pair(0)
        pl.when(jnp.logical_not(early))(project_query)
    else:
        project_query()
    for n in range(1, len(far)):
        far_scores(n)
    for n in range(1, len(far)):
        far_pair(n)
    c_wk.wait()
    c_wv.wait()
    c_xin.wait()
    c_inv.wait()
    if reach >= 1:

        @pl.when(takes_acc)
        def _():
            for g in range(kv_heads):
                acc_copy(g).wait_recv()
                part_v[g, :, :rows] += rcv[g, :HEAD_SIZE].astype(F32)
                part_k[g, :, :rows] += rcv[g, HEAD_SIZE:].astype(F32)

    for g in range(kv_heads):
        dk_low = (part_k[g, :, :rows] * scale).astype(BF)
        dv_low = part_v[g, :, :rows].astype(BF)
        dkv[head_cols(g), :] = dk_low
        dkv[head_cols(kv_heads + g), :] = dv_low
        both = dk_low.astype(F32) * k_t[g, :, :rows].astype(F32) + dv_low.astype(F32) * v_t[g]
        coupling = coupling + jnp.sum(both, axis=0, keepdims=True)

    def piece(n, at=0, size=width):
        return pacc[n, at : at + size] + dot(wkv[piece_rows(n, at, size), :], dkv[...], NN)

    lead = COUPLING_ROWS
    wide = jnp.broadcast_to(coupling, (lead, rows))

    def span_of(first, count=1):
        at, size = chunk[first][0], sum(chunk[n][1] for n in range(first, first + count))
        return (0, lead + size) if first == 0 else (lead + at, size)

    groups = chunk_groups(chunks)

    def a_copy(m):
        sl = pl.ds(*span_of(*groups[m]))
        return remote(rs_a.at[sl], rs_ar.at[sl], lsem.at[0], rs_rv.at[1 + m], {"tp": partner})

    send_c = remote(rs_c, rs_cr, lsem.at[1], rs_rv.at[0], {"tp": partner})
    base = 1 + len(groups)
    head = chunk[0][1]
    send_d = remote(rs_d, rs_dr, lsem.at[6], rs_rv.at[base + chunks], {"tp": diag})

    def b_copy(n):
        sl = pl.ds(*span_of(n))
        return remote(rs_b.at[sl], rs_br.at[sl], lsem.at[3], rs_rv.at[base + n], {"tp": cross})

    def x_copy(at, size):
        sl = pl.ds(at, size)
        if pipe_n == 1:
            return pltpu.make_async_copy(res.at[sl], out_h.at[sl], lsem.at[12])
        return remote(res.at[sl], out_h.at[sl], lsem.at[12], x_r, {"pipe": prev})

    def send_a(m):
        first, count = groups[m]
        at, size = chunk[first][0], sum(chunk[n][1] for n in range(first, first + count))
        rs_a[lead + at : lead + at + size, :] = piece(0, at, size).astype(BF)
        a_copy(m).start()

    send_a(0)
    rs_d[:lead, :] = wide.astype(BF)
    rs_d[lead:, :] = piece(0, 0, head).astype(BF)
    send_d.start()
    rs_b[:lead, :] = wide.astype(BF)
    rs_b[lead : lead + head, :] = piece(1, 0, head).astype(BF)
    b_copy(0).start()
    for m in range(1, len(groups)):
        send_a(m)
    for m, (first, count) in enumerate(groups):
        at, size = chunk[first][0], sum(chunk[n][1] for n in range(first, first + count))
        pacc[1, at : at + size] = piece(1, at, size)
        a_copy(m).wait_recv()
        for n in range(first, first + count):
            at, size = chunk[n]
            sl = slice(at, at + size)
            sh = slice(lead + at, lead + at + size)
            rs_b[sh, :] = (pacc[1, sl] + rs_ar[sh, :].astype(F32)).astype(BF)
            b_copy(n).start()
        if m == 0:
            rs_c[lead:, :] = piece(2).astype(BF)
            rs_c[:lead, :] = wide.astype(BF)
            send_c.start()
    pacc[3] = piece(3)
    iv = inv[...]
    send_c.wait_recv()
    for n in range(chunks):
        at, size = chunk[n]
        sl = slice(at, at + size)
        sh = slice(lead + at, lead + at + size)
        b_copy(n).wait_recv()
        normed = pacc[3, sl] + rs_cr[sh, :].astype(F32) + rs_br[sh, :].astype(F32)
        if n == 0:
            send_d.wait_recv()
            coup = coupling + rs_cr[:lead, :].astype(F32)[:1]
            coup = coup + rs_br[:lead, :].astype(F32)[:1] + rs_dr[:lead, :].astype(F32)[:1]
            drag = iv * coup / model_width
            normed = normed + rs_dr[lead:, :].astype(F32)
        val = gath[t, sl, :].astype(F32) + iv * (
            gain_col[sl, :] * normed - xin[sl, :].astype(F32) * drag
        )
        res[sl, :] = val.astype(BF)
        x_copy(at, size).start()

    shards = gath.at[pl.ds(0, 3)]
    remote(shards, shards, ag_s, ag_r.at[0], {"tp": partner}).wait_send()
    for d in range(1, reach + 1):

        @pl.when(sends_up(d))
        def _():
            both_blocks = kb.at[pl.ds(0, 2 * rows)]
            remote(
                both_blocks, both_blocks, kv_s.at[d - 1], k_r.at[d - 1], {"ctx": i + 1}
            ).wait_send()

    for n in range(len(far)):

        @pl.when(sends_far(n))
        def _():
            q_copy(n).wait_send()
            stat_copy(n).wait_send()
            remote(
                do_t, do_far.at[n], do_s.at[n], do_r.at[n, 0], {"ctx": i - far[n]}
            ).wait_send()

    if reach >= 1:

        @pl.when(sends_acc)
        def _():
            remote(snd, rcv, lsem.at[5], acc_r.at[0], {"ctx": i - 1}).wait_send()

    send_c.wait_send()
    send_d.wait_send()
    rest = pl.ds(lead + head, width - head)
    remote(
        rs_a.at[rest], rs_ar.at[rest], lsem.at[0], rs_rv.at[1], {"tp": partner}
    ).wait_send()
    remote(rs_b, rs_br, lsem.at[3], rs_rv.at[base], {"tp": cross}).wait_send()
    x_copy(0, width).wait()


def per_device(up, xin, inv, gain, q, k, v, ao, wq, wk, wv, wo, lens):
    ctx_n = lax.axis_size("ctx")
    pipe_n = lax.axis_size("pipe")
    tp_n = lax.axis_size("tp")
    assert tp_n == 4
    up, xin, q, k, v, ao = up[0].T, xin[0].T, q[0], k[0], v[0], ao[0]
    wq, wk, wv, wo = wq[0], wk[0], wv[0], wo[0]
    width, rows = up.shape
    reach = min((WINDOW - 2 + rows) // rows, ctx_n - 1)
    kv_cols, q_cols = k.shape[1], q.shape[1]
    kv_heads = kv_cols // HEAD_SIZE
    stacked = rows * (q_cols // kv_cols)
    chunks = len(chunk_cuts(width))
    groups = len(chunk_groups(chunks))
    parts = len(gather_cuts(width))
    vm = pltpu.VMEM
    dma = pltpu.SemaphoreType.DMA
    blocks = reach + 1
    own = min(reach, 1) + 1
    far = max(len(far_reach(reach)), 1)
    stats = -(-3 * kv_heads // 8) * 8
    scratch = [
        vm((tp_n, width, rows), BF),
        vm((width, rows), BF),
        vm(inv.shape, F32),
        vm(gain.shape, F32),
        vm(q.shape, BF),
        vm((blocks * rows, kv_cols), BF),
        vm((blocks * rows, kv_cols), BF),
        vm(ao.shape, BF),
        vm(wq.shape, BF),
        vm((wk.shape[0], 2 * kv_cols), BF),
        vm(wo.shape, BF),
        pltpu.SMEM(lens.shape, jnp.int32),
        vm((tp_n, wo.shape[0], width), BF),
        vm((width, rows), F32),
        vm((q_cols, rows), F32),
        vm((kv_heads, HEAD_SIZE, stacked), BF),
        vm((kv_heads, HEAD_SIZE, blocks * rows), BF),
        vm((kv_heads, HEAD_SIZE, stacked), BF),
        vm((stats, stacked), F32),
        vm((kv_heads, blocks * rows, stacked), F32),
        vm((kv_heads, blocks * rows, stacked), F32),
        vm((kv_heads, blocks * rows, stacked), BF),
        vm((far, kv_heads, HEAD_SIZE, stacked), BF),
        vm((far, kv_heads, HEAD_SIZE, stacked), BF),
        vm((far, stats, stacked), F32),
        vm((far, kv_heads, 2 * rows, stacked), F32),
        vm((kv_heads, HEAD_SIZE, own * rows), F32),
        vm((kv_heads, HEAD_SIZE, own * rows), F32),
        vm((q_cols, rows), BF),
        vm((2 * kv_cols, rows), BF),
        vm((kv_heads, HEAD_SIZE, rows), F32),
        vm((kv_heads, 2 * HEAD_SIZE, rows), BF),
        vm((kv_heads, 2 * HEAD_SIZE, rows), BF),
        vm((tp_n, width, rows), F32),
    ]
    scratch += [vm((COUPLING_ROWS + width, rows), BF)] * 6
    scratch += [vm((COUPLING_ROWS + chunk_cuts(width)[0][1], rows), BF)] * 2
    scratch += [vm((width, rows), BF)]
    scratch += [dma((13,))]
    scratch += [dma((max(reach, 1),))] * 3
    scratch += [dma(())]
    scratch += [dma((2 * parts + 1,))]
    scratch += [dma((far,))] * 2
    scratch += [dma((far,))]
    scratch += [dma((far, kv_heads))]
    scratch += [dma((far,))] * 2
    scratch += [dma((kv_heads,))]
    scratch += [pltpu.SemaphoreType.REGULAR] * 2
    scratch += [dma((2 + groups + chunks,))]
    scratch += [dma(())]
    out = pl.pallas_call(
        functools.partial(kernel, ctx_n, pipe_n, reach),
        out_shape=vm((width, rows), BF),
        in_specs=[pl.BlockSpec(memory_space=pl.ANY)] * 13,
        out_specs=pl.BlockSpec(memory_space=vm),
        scratch_shapes=scratch,
        compiler_params=pltpu.CompilerParams(collective_id=0, has_side_effects=True),
        name="layer_backward",
    )(up, xin, inv, gain, q, k, v, ao, wq, wk, wv, wo, lens)
    return out.T[None]


def solution(mesh):
    placed = (
        P("pipe", "ctx", "tp"),
        P("pipe", "ctx", "tp"),
        P("pipe", "ctx"),
        P("pipe", "tp"),
        P("pipe", "ctx", "tp"),
        P("pipe", "ctx", "tp"),
        P("pipe", "ctx", "tp"),
        P("pipe", "ctx", "tp"),
        P("pipe", None, "tp"),
        P("pipe", None, "tp"),
        P("pipe", None, "tp"),
        P("pipe", "tp", None),
        P("pipe"),
    )
    return jax.shard_map(
        per_device, mesh=mesh, in_specs=placed, out_specs=P("pipe", "ctx", "tp"), check_vma=False
    )
```
